128 devices in a mesh: dp: 4 (over z), ctx: 32 (over y, x, core).
Axes of the slice: x: 4, y: 4, z: 4, core: 2. Of those that a mesh axis runs over, the one named last changes fastest.
Arguments:
- source_picture_sequence: bfloat16 [4, 128, 8, 8, 16, 128], P('dp', 'ctx'), may hold values from -6 to 6
- slot_assignment: int32 [128], replicated, may hold values from 0 to 127, as said below
- segment_piece_counts: int32 [16], replicated, may hold values from 1 to 16, 128 in all
- logit_scaling: float32 [4], replicated, may hold values from 1 to 16
- filter_tap_coefficients: bfloat16 [3456, 256], replicated, may hold values from -0.109375 to 0.109375
- triple_linear_matrix: bfloat16 [256, 768], replicated, may hold values from -0.375 to 0.375
- final_linear_matrix: bfloat16 [256, 256], replicated, may hold values from -0.375 to 0.375
- upstream_gradient: bfloat16 [4, 128, 4, 128, 256], P('dp', 'ctx'), may hold values from -6 to 6
Outputs:
- latents: bfloat16 [4, 128, 4, 128, 256], P('dp', 'ctx')
- conv_grad: float32 [3456, 256], P('ctx')
The draws below stay inside these ranges and needn't reach their ends.
Inputs may be any that keep to these rules, and one draw needn't show every extreme that they name: `slot_assignment`: A permutation of the span numbers; entry i names the span at slot i, held by device i // 4. Each quarter of the span numbers, in order, fills one of the 4 positions on every device. The spans that follow one device's spans lie on at most two devices, at most two on any one device, and so do the spans that precede them; in every draw some device has two spans followed by spans on one other device.
All inputs are finite; a program needn't handle non-finite values.
Results may differ from the reference program's by a relative error of at most 0.0058.
Values may be sent and summed in bfloat16 or wider, within the bound.
A program may use at most 128 MiB of HBM per device.

```python
import math
import jax
import jax.numpy as jnp
import numpy as np
from jax import lax

C_IN = 128
C_OUT = 256
SLOTS = 4
FRAME_ROWS = 8
FRAME_COLS = 16
CLIP_MOST = 16
SPANS = 128
CLIPS = 16
CELLS = 128
PATCH = 3456
HEADS = 4
GROUPS = 4


def draw_slot_assignment(key, part):
    device_total = SPANS // SLOTS
    device_order = jax.random.permutation(key, device_total).astype(jnp.int32)
    position = jnp.argsort(device_order).astype(jnp.int32)
    reverse_position = device_total - 1 - position
    table = jnp.stack([position, device_total + position, 2 * device_total + reverse_position, 3 * device_total + reverse_position], axis=1)
    return table.reshape(-1).astype(jnp.int32)


def draw_logit_scaling(key, part):
    return jnp.exp(jax.random.uniform(key, (HEADS,), jnp.float32, math.log(1.0), math.log(12.0)))


def shard_levels(rng, dims, shards, smallest, top_value):
    def one(axis_at, shards_of):
        heights = jax.random.uniform(jax.random.fold_in(jax.random.fold_in(rng, 6), axis_at), (shards_of,), jnp.float32, smallest / len(shards), top_value / len(shards))
        return jnp.repeat(jnp.exp(heights), dims[axis_at] // shards_of).reshape((-1,) + (1,) * (len(dims) - axis_at - 1))

    gain = one(*shards[0])
    for cut in shards[1:]:
        gain = gain * one(*cut)
    return gain


def split_up(amount, total, limit, slope):
    loads = [(1 << 20) // math.isqrt(grade ** slope) + 1 for grade in range(2, amount + 1)]
    rest, holding = total - limit - (amount - 1), [1] * (amount - 1)
    while rest > 0:
        candidates = [i for i in range(amount - 1) if holding[i] < limit]
        mass, remaining = sum([loads[i] for i in candidates]), rest
        for i in candidates:
            extra = min(limit - holding[i], max(1, remaining * loads[i] // mass), rest)
            holding[i] = holding[i] + extra
            rest = rest - extra
    return np.array([limit] + holding)


def ragged_sizes(stream_key, number_of, total, most, skew):
    if number_of == 2:
        one = jax.random.randint(stream_key, (), max(1, total - most), min(most, total - 1) + 1)
        return jnp.stack([one, total - one])
    lengths = jnp.asarray(split_up(number_of, total, most, skew), jnp.int32)
    pairs = (number_of - 1) // 2
    source_of, sink = lengths[1:1 + 2 * pairs:2], lengths[2:2 + 2 * pairs:2]
    slack = jnp.minimum(source_of - 1, most - sink)
    shifted = jax.random.randint(jax.random.fold_in(stream_key, 1), (pairs,), 0, 1 << 20) % (slack + 1)
    lengths = lengths.at[1:1 + 2 * pairs:2].set(source_of - shifted).at[2:2 + 2 * pairs:2].set(sink + shifted)
    return lengths[jax.random.permutation(jax.random.fold_in(stream_key, 2), number_of)]


def centred(own_key, extent, width, reach, cuts=(), held_as=jnp.bfloat16):
    result = width * jax.random.normal(own_key, extent, jnp.float32)
    if cuts:
        result = result * shard_levels(own_key, extent, cuts, -0.22, 0.18)
    return jnp.clip(result, -reach, reach).astype(held_as)


def setup_inputs(seed: int = 0) -> dict:
    key_list = jax.random.split(jax.random.key(seed), 9)
    source_picture_sequence = centred(key_list[0], (GROUPS, SPANS, 8, FRAME_ROWS, FRAME_COLS, C_IN), 1.0, 6.0, ((0, 4), (1, 32)))
    slot_assignment = draw_slot_assignment(jax.random.fold_in(key_list[8], 71), 0)
    segment_piece_counts = ragged_sizes(key_list[2], CLIPS, SPANS, CLIP_MOST, 2).astype(jnp.int32)
    logit_scaling = draw_logit_scaling(jax.random.fold_in(key_list[8], 71), 0)
    filter_tap_coefficients = centred(key_list[4], (PATCH, C_OUT), PATCH ** -0.5, 0.109375)
    triple_linear_matrix = centred(key_list[5], (C_OUT, 3 * C_OUT), C_OUT ** -0.5, 0.375)
    final_linear_matrix = centred(key_list[6], (C_OUT, C_OUT), C_OUT ** -0.5, 0.375)
    upstream_gradient = centred(key_list[7], (GROUPS, SPANS, 4, CELLS, C_OUT), 1.0, 6.0, ((0, 4), (1, 32)))
    return {"source_picture_sequence": source_picture_sequence, "slot_assignment": slot_assignment, "segment_piece_counts": segment_piece_counts, "logit_scaling": logit_scaling, "filter_tap_coefficients": filter_tap_coefficients, "triple_linear_matrix": triple_linear_matrix, "final_linear_matrix": final_linear_matrix, "upstream_gradient": upstream_gradient}


masked_score = -1e+30

def clip_marks(segment_piece_counts, span_ids):
    clip_ends = jnp.cumsum(segment_piece_counts, dtype=jnp.int32)
    clip_starts = clip_ends - segment_piece_counts
    clip_index = lax.optimization_barrier(jnp.sum((span_ids[:, None] >= clip_ends[None, :]).astype(jnp.int32), axis=1, dtype=jnp.int32))
    opening = jnp.any(span_ids[:, None] == clip_starts[None, :], axis=1)
    return (clip_index, opening)

def conv_patches(frames):
    span_total, unused_len, rows_h, cols_w, channel_in = frames.shape
    padded = jnp.pad(frames, ((0, 0), (0, 0), (1, 1), (1, 1), (0, 0)))
    tap_list = []
    for step_t in range(3):
        for step_h in range(3):
            for step_w in range(3):
                tap_list.append(padded[:, step_t:step_t + 7:2, step_h:step_h + rows_h, step_w:step_w + cols_w, :])
    return jnp.concatenate(tap_list, axis=-1).reshape(-1, 27 * channel_in)

def timewise_softmax_mixing(grid_tile_entries, logit_scaling, triple_linear_matrix, final_linear_matrix, allowance_pattern):
    channel_width = grid_tile_entries.shape[-1]
    channel_group_index = logit_scaling.shape[0]
    head_size = channel_width // channel_group_index
    values32 = grid_tile_entries.astype(jnp.float32)
    normed = (values32 * lax.rsqrt(lax.optimization_barrier(jnp.mean(values32 * values32, axis=-1, keepdims=True)) + 1e-06)).astype(jnp.bfloat16)
    projected = jnp.einsum('gac,cd->gad', normed.astype(jnp.float32), triple_linear_matrix.astype(jnp.float32))
    head_shape = grid_tile_entries.shape[:2] + (channel_group_index, head_size)
    queries = projected[..., :channel_width].reshape(head_shape)
    keys_all = projected[..., channel_width:2 * channel_width].reshape(head_shape)
    head_values = projected[..., 2 * channel_width:].reshape(head_shape).astype(jnp.bfloat16)
    queries = queries * lax.rsqrt(lax.optimization_barrier(jnp.sum(queries * queries, axis=-1, keepdims=True)) + 1e-06)
    keys_all = keys_all * lax.rsqrt(lax.optimization_barrier(jnp.sum(keys_all * keys_all, axis=-1, keepdims=True)) + 1e-06)
    affinity_logits = jnp.einsum('gahd,gbhd->ghab', queries, keys_all, precision=lax.Precision.HIGHEST)
    affinity_logits = affinity_logits * logit_scaling[None, :, None, None]
    affinity_logits = jnp.where(allowance_pattern[None, None], affinity_logits, masked_score)
    highest = lax.optimization_barrier(jnp.max(affinity_logits, axis=-1, keepdims=True))
    weights = jnp.exp(affinity_logits - highest)
    probabilities = (weights / lax.optimization_barrier(jnp.sum(weights, axis=-1, keepdims=True))).astype(jnp.bfloat16)
    mixed_heads = jnp.einsum('ghab,gbhd->gahd', probabilities.astype(jnp.float32), head_values.astype(jnp.float32))
    mixed_heads = mixed_heads.astype(jnp.bfloat16).reshape(grid_tile_entries.shape)
    branch = jnp.einsum('gac,cd->gad', mixed_heads.astype(jnp.float32), final_linear_matrix.astype(jnp.float32))
    return (values32 + branch).astype(jnp.bfloat16)

def reference(source_picture_sequence, slot_assignment, segment_piece_counts, logit_scaling, filter_tap_coefficients, triple_linear_matrix, final_linear_matrix, upstream_gradient):
    span_ids = jnp.arange(SPANS, dtype=jnp.int32)
    clip_index, opening = clip_marks(segment_piece_counts, span_ids)
    slot_of_span = jnp.argsort(slot_assignment).astype(jnp.int32)
    frame_clip = jnp.repeat(clip_index, 4)
    frame_time = jnp.arange(SPANS * 4, dtype=jnp.int32)
    allowance_pattern = (frame_clip[:, None] == frame_clip[None, :]) & (frame_time[None, :] <= frame_time[:, None])
    conv_grad = jnp.zeros((PATCH, C_OUT), jnp.float32)
    results = []
    for group_idx in range(GROUPS):
        span_order = source_picture_sequence[group_idx][slot_of_span]
        previous = jnp.concatenate([jnp.zeros_like(span_order[:1, 6:]), span_order[:-1, 6:]], axis=0)
        previous = jnp.where(opening[:, None, None, None, None], jnp.zeros_like(previous), previous)
        patches = conv_patches(jnp.concatenate([previous, span_order], axis=1))
        conv_out = jnp.dot(patches, filter_tap_coefficients, preferred_element_type=jnp.float32).astype(jnp.bfloat16)
        grad_rows = upstream_gradient[group_idx][slot_of_span].reshape(-1, C_OUT)
        conv_grad = conv_grad + jnp.dot(patches.T, grad_rows, preferred_element_type=jnp.float32)
        location_entry_count = jnp.transpose(conv_out.reshape(SPANS * 4, CELLS, C_OUT), (1, 0, 2))
        blended_result = lax.map(lambda grid_tile_entries: timewise_softmax_mixing(grid_tile_entries[None], logit_scaling, triple_linear_matrix, final_linear_matrix, allowance_pattern)[0], location_entry_count)
        latent_spans = jnp.transpose(blended_result, (1, 0, 2)).reshape(SPANS, 4, CELLS, C_OUT)
        results.append(latent_spans[slot_assignment])
    return (jnp.stack(results), conv_grad)
```

```python
import jax
import jax.numpy as jnp
import numpy as np
from jax import lax
from jax.experimental import pallas as pl
from jax.experimental.pallas import tpu as pltpu
from jax.sharding import PartitionSpec as P

BF = jnp.bfloat16
F32 = jnp.float32
MESH = pl.DeviceIdType.MESH
DEV = 32
LOG2E = 1.4426950408889634


def one_hot_rows(rows, cols, pairs):
    table = np.zeros((rows, cols), np.float32)
    for row, col in pairs:
        table[row, col] = 1.0
    return jnp.asarray(table, BF)


def frame_rows():
    pairs = []
    for r in range(4):
        for qp in range(-1, 5):
            for k in range(4):
                for s in range(4):
                    q = qp + 4 * k
                    if 0 <= q < 16:
                        pairs.append((((r * 6 + qp + 1) * 4 + k) * 4 + s, (r * 4 + s) * 16 + q))
    return one_hot_rows(384, 256, pairs)


def gradient_rows():
    pairs = []
    for r in range(4):
        for qp in range(4):
            for k in range(4):
                for s in range(4):
                    pairs.append((((r * 4 + qp) * 4 + k) * 4 + s, (r * 4 + s) * 16 + qp + 4 * k))
    return one_hot_rows(256, 256, pairs)


def result_rows():
    pairs = []
    for qp in range(4):
        for k in range(4):
            for t in range(4):
                for s in range(4):
                    pairs.append(((s * 4 + t) * 16 + qp + 4 * k, ((qp * 4 + k) * 4 + t) * 4 + s))
    return one_hot_rows(256, 256, pairs)


def column_shifts():
    pairs = []
    for r in range(8):
        for k in range(4):
            for s in range(4):
                if k < 3:
                    pairs.append(((r * 4 + k) * 4 + s, (r * 4 + k + 1) * 4 + s))
                if k > 0:
                    pairs.append((128 + (r * 4 + k) * 4 + s, (r * 4 + k - 1) * 4 + s))
    return one_hot_rows(256, 128, pairs)


def slot_expand():
    pairs = []
    for e in range(32):
        for k in range(4):
            for s in range(4):
                pairs.append((4 * e + s, (e * 4 + k) * 4 + s))
    return one_hot_rows(128, 512, pairs)


def head_sums():
    table = np.kron(np.eye(4), np.ones((64, 64)))
    return jnp.asarray(table, BF)


def mm(a, b):
    return jnp.dot(a, b, preferred_element_type=F32)


def section_kernel(
    x_ref, w_ref, wqkv_ref, wout_ref, ug_ref, sa_ref, cnt_ref, scale_ref,
    px_ref, pg_ref, po_ref, sh_ref, ex_ref, hs_ref,
    out_ref, cg_ref,
    xp, xt, pat, t1r, t2s, t2r, cs, cr, gt, dw, gf, gbs, r1, s1b, acc1, r2, s2b, acc2, r3, s3b, acc3, r4, s4, r5,
    hot_t, hot_s, hot_u, mask, ys, qs, ks, vs, osb, rb, orv,
    send_sem, recv_sem, red_send, red_recv,
):
    z = lax.axis_index("dp")
    me = lax.axis_index("ctx")
    core = me % 2
    chip_x = (me // 2) % 4
    chip_y = me // 8

    barrier = pltpu.get_barrier_semaphore()

    def greet(step, carry):
        peer = (me + step) % DEV
        pl.semaphore_signal(barrier, inc=1, device_id={"ctx": peer}, device_id_type=MESH)
        return carry

    lax.fori_loop(1, DEV, greet, 0)
    for dz in range(1, 4):
        pl.semaphore_signal(barrier, inc=1, device_id={"dp": (z + dz) % 4}, device_id_type=MESH)

    def spread(source, target, phase):
        def one(step, carry):
            peer = (me + step) % DEV
            pltpu.make_async_remote_copy(
                src_ref=source(peer), dst_ref=target(me), send_sem=send_sem.at[phase],
                recv_sem=recv_sem.at[phase], device_id={"ctx": peer}, device_id_type=MESH,
            ).start()
            return carry

        lax.fori_loop(1, DEV, one, 0)

    def landed(view, phase):
        pltpu.make_async_copy(view, view, recv_sem.at[phase]).wait()

    def left(view, phase):
        pltpu.make_async_copy(view, view, send_sem.at[phase]).wait()

    zero_rows = jnp.zeros((8, 6, 16, 128), BF)
    xp[:, 0] = zero_rows
    xp[:, 9] = zero_rows
    xt[:, 0] = zero_rows[:2]
    xt[:, 9] = zero_rows[:2]
    px = px_ref[...]
    for pair in (3, 0, 1, 2):
        for g in range(2):
            rows = []
            for r in range(4 * g, 4 * g + 4):
                for s in range(4):
                    rows.append(
                        jnp.concatenate([x_ref[s, 2 * pair, r], x_ref[s, 2 * pair + 1, r]], axis=1)
                    )
            moved = mm(px, jnp.concatenate(rows, axis=0)).astype(BF)
            for f in range(2):
                xp[2 * pair + f, 1 + 4 * g : 5 + 4 * g] = moved[:, 128 * f : 128 * f + 128].reshape(4, 6, 16, 128)

    pl.semaphore_wait(barrier, DEV - 1 + 3)

    my_r, my_q = me // 4, me % 4
    spread(
        lambda peer: xp.at[pl.ds(6, 2), peer // 4 + 1, peer % 4 + 1],
        lambda mine: t1r.at[:, mine],
        0,
    )
    t1r[:, me] = xp[6:8, my_r + 1, my_q + 1]

    sa = sa_ref[...].astype(F32)
    opening = jnp.zeros((1, 128), jnp.bool_)
    first = jnp.int32(0)
    for n in range(16):
        opening = opening | (sa == first.astype(F32))
        first = first + cnt_ref[n]
    wanted = jnp.where(opening, -1000.0, sa * 4.0 - 4.0)
    codes = jnp.concatenate([sa * 4.0, wanted, jnp.zeros((14, 128), F32)], axis=0).astype(BF)
    wide = mm(codes, ex_ref[...])
    lane = lax.broadcasted_iota(jnp.int32, (1, 512), 1)
    kpat = ((lane >> 2) & 3).astype(F32)
    vrow = wide[0:1] + kpat
    wrow = wide[1:2] + kpat
    vcol = jnp.transpose(jnp.broadcast_to(vrow, (128, 512)))
    wcol = jnp.transpose(jnp.broadcast_to(wrow, (128, 512)))
    lane128 = lax.broadcasted_iota(jnp.int32, (1, 128), 1).astype(F32)
    for j in range(4):
        cols = slice(128 * j, 128 * j + 128)
        hot_t[:, cols] = jnp.where(wcol == vrow[:, cols], 1.0, 0.0).astype(BF)
        hot_u[:, cols] = jnp.where(vcol == lane128 * 4.0 + j, 1.0, 0.0).astype(BF)
        ids = lax.broadcasted_iota(jnp.int32, (128, 1), 0).astype(F32) * 4.0 + j
        hot_s[cols, :] = jnp.where(ids == vrow, 1.0, 0.0).astype(BF)

    def taps(t, tail):
        for kt in range(3):
            for kh in range(3):
                for kw in range(3):
                    tap = (kt * 3 + kh) * 3 + kw
                    if tail and kt < 2:
                        tile = xt[kt, kh : kh + 8, kw : kw + 4]
                    else:
                        tile = xp[2 * t - 2 + kt, kh : kh + 8, kw : kw + 4]
                    pat[pl.ds(512 * t, 512), 128 * tap : 128 * tap + 128] = tile.reshape(512, 128)

    def convolve(t):
        for half in range(2):
            rows = pat[pl.ds(512 * t + 256 * half, 256), :]
            cs[pl.ds(16 * half, 16), t] = mm(rows, w_ref[...]).astype(BF).reshape(16, 16, 256)

    def conv_frame(t, tail):
        taps(t, tail)
        convolve(t)
        spread(lambda peer: cs.at[peer, t], lambda mine: cr.at[mine, t], 2 + t)
        cr[me, t] = cs[me, t]

    def later(t, carry):
        conv_frame(t, False)
        return carry

    lax.fori_loop(1, 4, later, 0)

    landed(t1r.at[:, pl.ds(0, DEV - 1)], 0)
    both = jnp.concatenate([t1r[0].reshape(512, 128), t1r[1].reshape(512, 128)], axis=1)
    moved = mm(hot_t[...], both).astype(BF)
    t2s[0] = moved[:, :128].reshape(32, 16, 128)
    t2s[1] = moved[:, 128:].reshape(32, 16, 128)
    spread(lambda peer: t2s.at[:, peer], lambda mine: t2r.at[:, mine], 1)
    t2r[:, me] = t2s[:, me]

    pg = pg_ref[...]
    for t in range(4):
        for g in range(2):
            rows = []
            for r in range(4 * g, 4 * g + 4):
                for s in range(4):
                    rows.append(ug_ref[s, t, 16 * r : 16 * r + 16])
            moved = mm(pg, jnp.concatenate(rows, axis=0))
            at = (2 * t + g) * 256
            gt[:, at : at + 256] = jnp.transpose(moved).astype(BF)

    landed(t2r.at[:, pl.ds(0, DEV - 1)], 1)
    for f in range(2):
        tiles = t2r[f].reshape(8, 4, 16, 128)
        xt[f, 1:9, 1:5] = tiles
        up = mm(sh_ref[0:128], tiles[:, 0].reshape(128, 128)).astype(BF)
        down = mm(sh_ref[128:256], tiles[:, 3].reshape(128, 128)).astype(BF)
        xt[f, 1:9, 5] = up.reshape(8, 16, 128)
        xt[f, 1:9, 0] = down.reshape(8, 16, 128)
    conv_frame(0, True)

    def grad_block(n, carry):
        at = pl.multiple_of(n * 256, 256)
        part = mm(gt[...], pat[:, pl.ds(at, 256)])
        dw[pl.ds(at, 256), :] = jnp.transpose(part)
        return carry

    lax.fori_loop(0, 13, grad_block, 0)
    dw[3328:3456, :] = jnp.transpose(mm(gt[...], pat[:, 3328:3456]))
    dw[3456:3464, :] = jnp.zeros((8, 256), F32)

    def regroup(g, carry):
        block = dw[pl.ds(pl.multiple_of(216 * g, 8), 224), :]
        for j in range(8):
            gf[j // 4, j % 4, g] = block[27 * j : 27 * j + 32]
        return carry

    lax.fori_loop(0, 16, regroup, 0)
    for part in range(4):
        gbs[part] = gf[1 - core, part].astype(BF)
    partner = me + 1 - 2 * core

    def reduce_copy(source, target, index, where):
        return pltpu.make_async_remote_copy(
            src_ref=source, dst_ref=target, send_sem=red_send.at[index],
            recv_sem=red_recv.at[index], device_id=where, device_id_type=MESH,
        )

    core_copy = reduce_copy(gbs, r1, 12, {"ctx": partner})
    core_copy.start()

    def see(a, carry):
        row = lax.broadcasted_iota(jnp.int32, (128, 192), 0)
        col = lax.broadcasted_iota(jnp.int32, (128, 192), 1)
        span = 32 * a + (row & 31)
        when = span * 4 + (row >> 5)
        col_t = (col >= 48).astype(jnp.int32) + (col >= 96).astype(jnp.int32) + (col >= 144).astype(jnp.int32)
        other = 32 * a - 16 + col - 48 * col_t
        start = jnp.zeros((128, 192), jnp.int32)
        total = jnp.int32(0)
        for n in range(15):
            total = total + cnt_ref[n]
            start = jnp.where(span >= total, total, start)
        seen = (other >= start) & (other * 4 + col_t <= when)
        mask[a] = jnp.where(seen, 1.0, 0.0).astype(BF)
        return carry

    lax.fori_loop(0, 4, see, 0)
    ks[:, 0:16] = jnp.zeros((4, 16, 256), BF)
    vs[:, 0:16] = jnp.zeros((4, 16, 256), BF)

    for t in (1, 2, 3, 0):
        landed(cr.at[pl.ds(0, DEV - 1), t], 2 + t)
        sorted_rows = mm(hot_s[...], cr[:, t].reshape(512, 256)).astype(BF)
        for k in range(4):
            ys[k, t] = sorted_rows[128 * k : 128 * k + 128]

    lanes = lax.broadcasted_iota(jnp.int32, (1, 256), 1)
    heads = [(lanes >> 6) == h for h in range(4)]
    scale = jnp.zeros((1, 256), F32)
    for h in range(4):
        scale = jnp.where(heads[h], scale_ref[h] * LOG2E, scale)

    def cell(k):
        rows = jnp.concatenate([ys[k, t] for t in range(4)], axis=0)
        wide = rows.astype(F32)
        mean = jnp.mean(wide * wide, axis=1, keepdims=True)
        normed = (wide * lax.rsqrt(mean + 1e-6)).astype(BF)
        query = mm(normed, wqkv_ref[:, 0:256])
        sums = mm((query * query).astype(BF), hs_ref[...])
        query = (query * (lax.rsqrt(sums + 1e-6) * scale)).astype(BF)
        key = mm(normed, wqkv_ref[:, 256:512])
        sums = mm((key * key).astype(BF), hs_ref[...])
        key = (key * lax.rsqrt(sums + 1e-6)).astype(BF)
        value = mm(normed, wqkv_ref[:, 512:768]).astype(BF)
        for t in range(4):
            qs[t] = query[128 * t : 128 * t + 128]
            ks[t, 16:144] = key[128 * t : 128 * t + 128]
            vs[t, 16:144] = value[128 * t : 128 * t + 128]

        def tile(a, carry):
            at = pl.multiple_of(32 * a, 32)
            qa = jnp.concatenate([qs[t, pl.ds(at, 32)] for t in range(4)], axis=0)
            zero = jnp.zeros_like(qa)
            stacked = jnp.concatenate([jnp.where(heads[h], qa, zero) for h in range(4)], axis=0)
            keys = jnp.concatenate([ks[t, pl.ds(at, 48)] for t in range(4)], axis=0)
            vals = jnp.concatenate([vs[t, pl.ds(at, 48)] for t in range(4)], axis=0)
            scores = lax.dot_general(
                stacked, keys, (((1,), (1,)), ((), ())), preferred_element_type=F32
            )
            see_a = mask[a]
            weights = jnp.exp2(scores).astype(BF) * jnp.concatenate([see_a] * 4, axis=0)
            total = jnp.sum(weights.astype(F32), axis=1, keepdims=True)
            mixed = mm(weights, vals) / total
            joined = jnp.zeros((128, 256), F32)
            for h in range(4):
                joined = jnp.where(heads[h], mixed[128 * h : 128 * h + 128], joined)
            base = jnp.concatenate([ys[k, t, pl.ds(at, 32)] for t in range(4)], axis=0)
            done = (base.astype(F32) + mm(joined.astype(BF), wout_ref[...])).astype(BF)
            for t in range(4):
                osb[t, pl.ds(at, 32)] = done[32 * t : 32 * t + 32]
            return carry

        lax.fori_loop(0, 4, tile, 0)
        back = mm(hot_u[...], osb[...].reshape(512, 256)).astype(BF)
        rb[k] = back.reshape(32, 16, 256)
        spread(lambda peer: rb.at[k, peer], lambda mine: orv.at[mine, k], 6 + k)
        orv[me, k] = rb[k, me]

    cell(0)
    core_copy.wait()
    for part in range(4):
        s1b[part] = (gf[core, part] + r1[part].astype(F32)).astype(BF)
    acc1[...] = gf[core, z] + r1[z].astype(F32)
    z_copies = [
        reduce_copy(s1b.at[(z + d) % 4], r2.at[d - 1], d - 1, {"dp": (z + d) % 4}) for d in (1, 2, 3)
    ]
    for copy in z_copies:
        copy.start()
    cell(1)
    cell(2)
    for copy in z_copies:
        copy.wait()
    acc2[...] = acc1[...] + r2[0].astype(F32) + r2[1].astype(F32) + r2[2].astype(F32)
    s2b[...] = acc2[...].astype(BF)
    y_copies = []
    for d in (1, 2, 3):
        yp = (chip_y + d) % 4
        y_copies.append(
            reduce_copy(s2b.at[pl.ds(yp * 4, 4)], r3.at[d - 1], 2 + d, {"ctx": (yp * 4 + chip_x) * 2 + core})
        )
    for copy in y_copies:
        copy.start()
    cell(3)
    for copy in y_copies:
        copy.wait()
    acc3[...] = acc2[pl.ds(chip_y * 4, 4)] + r3[0].astype(F32) + r3[1].astype(F32) + r3[2].astype(F32)
    s3b[...] = acc3[...].astype(BF)
    x_copies = []
    for d in (1, 2, 3):
        xq = (chip_x + d) % 4
        x_copies.append(
            reduce_copy(s3b.at[xq], r4.at[d - 1], 5 + d, {"ctx": (chip_y * 4 + xq) * 2 + core})
        )
    for copy in x_copies:
        copy.start()
    for copy in x_copies:
        copy.wait()
    s4[...] = acc3[chip_x] + r4[0].astype(F32) + r4[1].astype(F32) + r4[2].astype(F32)
    end_copies = [
        reduce_copy(s4, r5.at[z], 8 + d, {"dp": (z + d) % 4}) for d in (1, 2, 3)
    ]
    for copy in end_copies:
        copy.start()
    r5[z] = s4[...]

    for k in range(4):
        landed(orv.at[pl.ds(0, DEV - 1), k], 6 + k)
    po = po_ref[...]
    for r in range(8):
        rows = orv[4 * r : 4 * r + 4].reshape(256, 256)
        moved = mm(po, rows).astype(BF)
        for s in range(4):
            for t in range(4):
                at = (s * 4 + t) * 16
                out_ref[s, t, 16 * r : 16 * r + 16] = moved[at : at + 16]
    for copy in end_copies:
        copy.wait()
    for part in range(4):
        cg_ref[27 * part : 27 * part + 27] = r5[part, 0:27]

    left(t1r.at[:, pl.ds(0, DEV - 1)], 0)
    left(t2s.at[:, pl.ds(0, DEV - 1)], 1)
    for t in range(4):
        left(cs.at[pl.ds(0, DEV - 1), t], 2 + t)
    for k in range(4):
        left(rb.at[k, pl.ds(0, DEV - 1)], 6 + k)


def per_device(pictures, slots, counts, scaling, taps, triple, final, upstream):
    vm = lambda shape, kind: pltpu.VMEM(shape, kind)
    scratch = [
        vm((8, 10, 6, 16, 128), BF),
        vm((2, 10, 6, 16, 128), BF),
        vm((2048, 3456), BF),
        vm((2, 32, 16, 128), BF),
        vm((2, 32, 16, 128), BF),
        vm((2, 32, 16, 128), BF),
        vm((32, 4, 16, 256), BF),
        vm((32, 4, 16, 256), BF),
        vm((256, 2048), BF),
        vm((3464, 256), F32),
        vm((2, 4, 16, 32, 256), F32),
        vm((4, 16, 32, 256), BF),
        vm((4, 16, 32, 256), BF),
        vm((4, 16, 32, 256), BF),
        vm((16, 32, 256), F32),
        vm((3, 16, 32, 256), BF),
        vm((16, 32, 256), BF),
        vm((16, 32, 256), F32),
        vm((3, 4, 32, 256), BF),
        vm((4, 32, 256), BF),
        vm((4, 32, 256), F32),
        vm((3, 32, 256), BF),
        vm((32, 256), F32),
        vm((4, 32, 256), F32),
        vm((512, 512), BF),
        vm((512, 512), BF),
        vm((512, 512), BF),
        vm((4, 128, 192), BF),
        vm((4, 4, 128, 256), BF),
        vm((4, 128, 256), BF),
        vm((4, 144, 256), BF),
        vm((4, 144, 256), BF),
        vm((4, 128, 256), BF),
        vm((4, 32, 16, 256), BF),
        vm((32, 4, 16, 256), BF),
        pltpu.SemaphoreType.DMA((10,)),
        pltpu.SemaphoreType.DMA((10,)),
        pltpu.SemaphoreType.DMA((13,)),
        pltpu.SemaphoreType.DMA((13,)),
    ]
    v = pl.BlockSpec(memory_space=pltpu.VMEM)
    s = pl.BlockSpec(memory_space=pltpu.SMEM)
    latents, conv_grad = pl.pallas_call(
        section_kernel,
        out_shape=(
            jax.ShapeDtypeStruct((4, 4, 128, 256), BF),
            jax.ShapeDtypeStruct((108, 256), F32),
        ),
        in_specs=[v, v, v, v, v, v, s, s, v, v, v, v, v, v],
        out_specs=(v, v),
        scratch_shapes=scratch,
        compiler_params=pltpu.CompilerParams(
            collective_id=0, has_side_effects=True, vmem_limit_bytes=62 * 1024 * 1024
        ),
    )(
        pictures[0], taps, triple, final, upstream[0], slots.reshape(1, 128), counts, scaling,
        frame_rows(), gradient_rows(), result_rows(), column_shifts(), slot_expand(), head_sums(),
    )
    return latents[None], conv_grad


def solution(mesh):
    placed = (
        P("dp", "ctx", None, None, None, None),
        P(), P(), P(), P(), P(), P(),
        P("dp", "ctx", None, None, None),
    )
    return jax.shard_map(
        per_device,
        mesh=mesh,
        in_specs=placed,
        out_specs=(P("dp", "ctx", None, None, None), P("ctx", None)),
        check_vma=False,
    )
```

```python
import jax
import jax.numpy as jnp
import numpy as np
from jax import lax
from jax.experimental import pallas as pl
from jax.experimental.pallas import tpu as pltpu
from jax.sharding import PartitionSpec as P

BF = jnp.bfloat16
F32 = jnp.float32
MESH = pl.DeviceIdType.MESH
DEV = 32
LOG2E = 1.4426950408889634


def one_hot_rows(rows, cols, pairs):
    table = np.zeros((rows, cols), np.float32)
    for row, col in pairs:
        table[row, col] = 1.0
    return jnp.asarray(table, BF)


def frame_rows():
    pairs = []
    for r in range(4):
        for qp in range(-1, 5):
            for k in range(4):
                for s in range(4):
                    q = qp + 4 * k
                    if 0 <= q < 16:
                        pairs.append((((r * 6 + qp + 1) * 4 + k) * 4 + s, (r * 4 + s) * 16 + q))
    return one_hot_rows(384, 256, pairs)


def gradient_rows():
    pairs = []
    for r in range(4):
        for qp in range(4):
            for k in range(4):
                for s in range(4):
                    pairs.append((((r * 4 + qp) * 4 + k) * 4 + s, (r * 4 + s) * 16 + qp + 4 * k))
    return one_hot_rows(256, 256, pairs)


def result_rows():
    pairs = []
    for qp in range(4):
        for k in range(4):
            for t in range(4):
                for s in range(4):
                    pairs.append(((s * 4 + t) * 16 + qp + 4 * k, ((qp * 4 + k) * 4 + t) * 4 + s))
    return one_hot_rows(256, 256, pairs)


def column_shifts():
    pairs = []
    for r in range(8):
        for k in range(4):
            for s in range(4):
                if k < 3:
                    pairs.append(((r * 4 + k) * 4 + s, (r * 4 + k + 1) * 4 + s))
                if k > 0:
                    pairs.append((128 + (r * 4 + k) * 4 + s, (r * 4 + k - 1) * 4 + s))
    return one_hot_rows(256, 128, pairs)


def slot_expand():
    pairs = []
    for e in range(32):
        for k in range(4):
            for s in range(4):
                pairs.append((4 * e + s, (e * 4 + k) * 4 + s))
    return one_hot_rows(128, 512, pairs)


def head_sums():
    table = np.kron(np.eye(4), np.ones((64, 64)))
    return jnp.asarray(table, BF)


def mm(a, b):
    return jnp.dot(a, b, preferred_element_type=F32)


def section_kernel(
    x_hbm, w_hbm, wqkv_hbm, wout_hbm, ug_hbm, sa_ref, cnt_ref, scale_ref,
    px_hbm, pg_hbm, po_hbm, sh_hbm, ex_hbm, hs_hbm,
    out_ref, cg_ref,
    x_ref, px_ref, ug_ref, pg_ref, w_ref, ex_ref, sh_ref, wqkv_ref, hs_ref, wout_ref, po_ref,
    xp, xt, pat, t1r, t2s, t2r, cs, cr, gt, dwt, dw, gf, gbs, r1, s1b, zu, zd, acc2, s2b, r3, s3b, acc3, r4, s4, r5,
    hot_t, hot_s, hot_u, mask, ys, qs, ks, vs, osb, rb, orv,
    send_sem, recv_sem, red_send, red_recv, in_sem,
):
    z = lax.axis_index("dp")
    me = lax.axis_index("ctx")
    core = me & 1
    chip_x = (me >> 1) & 3
    chip_y = me >> 3

    loads = [
        pltpu.make_async_copy(source, target, in_sem.at[n])
        for n, (source, target) in enumerate((
            (x_hbm, x_ref), (px_hbm, px_ref), (ug_hbm, ug_ref), (pg_hbm, pg_ref), (w_hbm, w_ref), (ex_hbm, ex_ref),
            (sh_hbm, sh_ref), (wqkv_hbm, wqkv_ref), (hs_hbm, hs_ref), (wout_hbm, wout_ref), (po_hbm, po_ref),
        ))
    ]
    for load in loads:
        load.start()

    barrier = pltpu.get_barrier_semaphore()

    def greet(step, carry):
        peer = (me + step) & (DEV - 1)
        pl.semaphore_signal(barrier, inc=1, device_id={"ctx": peer}, device_id_type=MESH)
        return carry

    lax.fori_loop(1, DEV, greet, 0)
    for dz in range(1, 4):
        pl.semaphore_signal(barrier, inc=1, device_id={"dp": (z + dz) & 3}, device_id_type=MESH)

    def spread(source, target, phase):
        def one(step, carry):
            peer = (me + step) & (DEV - 1)
            pltpu.make_async_remote_copy(
                src_ref=source(peer), dst_ref=target(me), send_sem=send_sem.at[phase],
                recv_sem=recv_sem.at[phase], device_id={"ctx": peer}, device_id_type=MESH,
            ).start()
            return carry

        lax.fori_loop(1, DEV, one, 0)

    def landed(view, phase):
        pltpu.make_async_copy(view, view, recv_sem.at[phase]).wait()

    def left(view, phase):
        pltpu.make_async_copy(view, view, send_sem.at[phase]).wait()

    zero_rows = jnp.zeros((8, 6, 16, 128), BF)
    xp[:, 0] = zero_rows
    xp[:, 9] = zero_rows
    xt[:, 0] = zero_rows[:2]
    xt[:, 9] = zero_rows[:2]
    loads[0].wait()
    loads[1].wait()
    px = px_ref[...]
    for pair in (3, 0, 1, 2):
        for g in range(2):
            rows = []
            for r in range(4 * g, 4 * g + 4):
                for s in range(4):
                    rows.append(
                        jnp.concatenate([x_ref[s, 2 * pair, r], x_ref[s, 2 * pair + 1, r]], axis=1)
                    )
            moved = mm(px, jnp.concatenate(rows, axis=0)).astype(BF)
            for f in range(2):
                xp[2 * pair + f, 1 + 4 * g : 5 + 4 * g] = moved[:, 128 * f : 128 * f + 128].reshape(4, 6, 16, 128)

    def taps(t, tail, kts):
        for kt in kts:
            for kh in range(3):
                for kw in range(3):
                    tap = (kt * 3 + kh) * 3 + kw
                    if tail:
                        tile = xt[kt, kh : kh + 8, kw : kw + 4]
                    else:
                        tile = xp[2 * t - 2 + kt, kh : kh + 8, kw : kw + 4]
                    pat[pl.ds(512 * t, 512), 128 * tap : 128 * tap + 128] = tile.reshape(512, 128)

    def convolve(t):
        for half in range(2):
            rows = pat[pl.ds(512 * t + 256 * half, 256), :]
            cs[pl.ds(16 * half, 16), t] = mm(rows, w_ref[...]).astype(BF).reshape(16, 16, 256)
        cr[me, t] = cs[me, t]

    def send_frame(t):
        spread(lambda peer: cs.at[peer, t], lambda mine: cr.at[mine, t], 2 + t)

    loads[4].wait()
    taps(1, False, (0, 1, 2))
    convolve(1)
    loads[2].wait()
    loads[3].wait()
    pg = pg_ref[...]
    for t in range(4):
        for g in range(2):
            rows = []
            for r in range(4 * g, 4 * g + 4):
                for s in range(4):
                    rows.append(ug_ref[s, t, 16 * r : 16 * r + 16])
            moved = mm(pg, jnp.concatenate(rows, axis=0))
            at = (2 * t + g) * 256
            gt[:, at : at + 256] = jnp.transpose(moved).astype(BF)
    pl.semaphore_wait(barrier, DEV - 1 + 3)

    my_r, my_q = me >> 2, me & 3
    spread(
        lambda peer: xp.at[pl.ds(6, 2), (peer >> 2) + 1, (peer & 3) + 1],
        lambda mine: t1r.at[:, mine],
        0,
    )
    send_frame(1)
    t1r[:, me] = xp[6:8, my_r + 1, my_q + 1]

    def later(t, carry):
        taps(t, False, (0, 1, 2))
        convolve(t)
        return carry

    lax.fori_loop(2, 4, later, 0)
    taps(0, False, (2,))

    loads[5].wait()
    sa = sa_ref[...].astype(F32)
    opening = jnp.zeros((1, 128), jnp.bool_)
    first = jnp.int32(0)
    for n in range(16):
        opening = opening | (sa == first.astype(F32))
        first = first + cnt_ref[n]
    wanted = jnp.where(opening, -1000.0, sa * 4.0 - 4.0)
    codes = jnp.concatenate([sa * 4.0, wanted, jnp.zeros((14, 128), F32)], axis=0).astype(BF)
    wide = mm(codes, ex_ref[...])
    lane = lax.broadcasted_iota(jnp.int32, (1, 512), 1)
    kpat = ((lane >> 2) & 3).astype(F32)
    vrow = wide[0:1] + kpat
    wrow = wide[1:2] + kpat
    vcol = jnp.transpose(jnp.broadcast_to(vrow, (128, 512)))
    wcol = jnp.transpose(jnp.broadcast_to(wrow, (128, 512)))
    lane128 = lax.broadcasted_iota(jnp.int32, (1, 128), 1).astype(F32)
    for j in range(4):
        cols = slice(128 * j, 128 * j + 128)
        hot_t[:, cols] = jnp.where(wcol == vrow[:, cols], 1.0, 0.0).astype(BF)
        hot_u[:, cols] = jnp.where(vcol == lane128 * 4.0 + j, 1.0, 0.0).astype(BF)
        ids = lax.broadcasted_iota(jnp.int32, (128, 1), 0).astype(F32) * 4.0 + j
        hot_s[cols, :] = jnp.where(ids == vrow, 1.0, 0.0).astype(BF)

    def grad_last(n, carry):
        at = pl.multiple_of(2304 + n * 256, 256)
        dw[pl.ds(at, 256), :] = jnp.transpose(mm(gt[...], pat[:, pl.ds(at, 256)]))
        return carry

    lax.fori_loop(0, 4, grad_last, 0)
    dw[3328:3456, :] = jnp.transpose(mm(gt[...], pat[:, 3328:3456]))
    dw[3456:3464, :] = jnp.zeros((8, 256), F32)

    landed(t1r.at[:, pl.ds(0, DEV - 1)], 0)
    both = jnp.concatenate([t1r[0].reshape(512, 128), t1r[1].reshape(512, 128)], axis=1)
    moved = mm(hot_t[...], both).astype(BF)
    t2s[0] = moved[:, :128].reshape(32, 16, 128)
    t2s[1] = moved[:, 128:].reshape(32, 16, 128)
    spread(lambda peer: t2s.at[:, peer], lambda mine: t2r.at[:, mine], 1)
    t2r[:, me] = t2s[:, me]
    send_frame(2)
    send_frame(3)

    def grad_main(n, carry):
        at = pl.multiple_of(n * 256, 256)
        dwt[:, pl.ds(at, 256)] = mm(gt[:, 512:2048], pat[512:2048, pl.ds(at, 256)])
        return carry

    lax.fori_loop(0, 9, grad_main, 0)

    landed(t2r.at[:, pl.ds(0, DEV - 1)], 1)
    loads[6].wait()
    for f in range(2):
        tiles = t2r[f].reshape(8, 4, 16, 128)
        xt[f, 1:9, 1:5] = tiles
        up = mm(sh_ref[0:128], tiles[:, 0].reshape(128, 128)).astype(BF)
        down = mm(sh_ref[128:256], tiles[:, 3].reshape(128, 128)).astype(BF)
        xt[f, 1:9, 5] = up.reshape(8, 16, 128)
        xt[f, 1:9, 0] = down.reshape(8, 16, 128)
    taps(0, True, (0, 1))
    convolve(0)
    send_frame(0)

    def grad_tail(n, carry):
        at = pl.multiple_of(n * 256, 256)
        part = dwt[:, pl.ds(at, 256)] + mm(gt[:, 0:512], pat[0:512, pl.ds(at, 256)])
        dw[pl.ds(at, 256), :] = jnp.transpose(part)
        return carry

    lax.fori_loop(0, 9, grad_tail, 0)
    def regroup(g, carry):
        block = dw[pl.ds(pl.multiple_of(216 * g, 8), 224), :]
        for j in range(8):
            gf[j // 4, j % 4, g] = block[27 * j : 27 * j + 32]
        return carry

    lax.fori_loop(0, 16, regroup, 0)
    for part in range(4):
        gbs[part] = gf[1 - core, part].astype(BF)
    partner = me + 1 - 2 * core

    def reduce_copy(source, target, index, where):
        return pltpu.make_async_remote_copy(
            src_ref=source, dst_ref=target, send_sem=red_send.at[index],
            recv_sem=red_recv.at[index], device_id=where, device_id_type=MESH,
        )

    core_copy = reduce_copy(gbs, r1, 0, {"ctx": partner})
    core_copy.start()

    def see(a, carry):
        row = lax.broadcasted_iota(jnp.int32, (128, 192), 0)
        col = lax.broadcasted_iota(jnp.int32, (128, 192), 1)
        span = 32 * a + (row & 31)
        when = span * 4 + (row >> 5)
        col_t = (col >= 48).astype(jnp.int32) + (col >= 96).astype(jnp.int32) + (col >= 144).astype(jnp.int32)
        other = 32 * a - 16 + col - 48 * col_t
        start = jnp.zeros((128, 192), jnp.int32)
        total = jnp.int32(0)
        for n in range(15):
            total = total + cnt_ref[n]
            start = jnp.where(span >= total, total, start)
        seen = (other >= start) & (other * 4 + col_t <= when)
        mask[a] = jnp.where(seen, 1.0, 0.0).astype(BF)
        return carry

    lax.fori_loop(0, 4, see, 0)
    ks[:, 0:16] = jnp.zeros((4, 16, 256), BF)
    vs[:, 0:16] = jnp.zeros((4, 16, 256), BF)

    for t in (1, 2, 3, 0):
        landed(cr.at[pl.ds(0, DEV - 1), t], 2 + t)
        sorted_rows = mm(hot_s[...], cr[:, t].reshape(512, 256)).astype(BF)
        for k in range(4):
            ys[k, t] = sorted_rows[128 * k : 128 * k + 128]

    for load in loads[7:10]:
        load.wait()
    lanes = lax.broadcasted_iota(jnp.int32, (1, 256), 1)
    heads = [(lanes >> 6) == h for h in range(4)]
    scale = jnp.zeros((1, 256), F32)
    for h in range(4):
        scale = jnp.where(heads[h], scale_ref[h] * LOG2E, scale)

    def cell(k):
        rows = jnp.concatenate([ys[k, t] for t in range(4)], axis=0)
        wide = rows.astype(F32)
        mean = jnp.mean(wide * wide, axis=1, keepdims=True)
        normed = (wide * lax.rsqrt(mean + 1e-6)).astype(BF)
        query = mm(normed, wqkv_ref[:, 0:256])
        sums = mm((query * query).astype(BF), hs_ref[...])
        query = (query * (lax.rsqrt(sums + 1e-6) * scale)).astype(BF)
        key = mm(normed, wqkv_ref[:, 256:512])
        sums = mm((key * key).astype(BF), hs_ref[...])
        key = (key * lax.rsqrt(sums + 1e-6)).astype(BF)
        value = mm(normed, wqkv_ref[:, 512:768]).astype(BF)
        for t in range(4):
            qs[t] = query[128 * t : 128 * t + 128]
            ks[t, 16:144] = key[128 * t : 128 * t + 128]
            vs[t, 16:144] = value[128 * t : 128 * t + 128]

        def tile(a, carry):
            at = pl.multiple_of(32 * a, 32)
            qa = jnp.concatenate([qs[t, pl.ds(at, 32)] for t in range(4)], axis=0)
            zero = jnp.zeros_like(qa)
            stacked = jnp.concatenate([jnp.where(heads[h], qa, zero) for h in range(4)], axis=0)
            keys = jnp.concatenate([ks[t, pl.ds(at, 48)] for t in range(4)], axis=0)
            vals = jnp.concatenate([vs[t, pl.ds(at, 48)] for t in range(4)], axis=0)
            scores = lax.dot_general(
                stacked, keys, (((1,), (1,)), ((), ())), preferred_element_type=F32
            )
            see_a = mask[a]
            weights = jnp.exp2(scores).astype(BF) * jnp.concatenate([see_a] * 4, axis=0)
            total = jnp.sum(weights.astype(F32), axis=1, keepdims=True)
            mixed = mm(weights, vals) / total
            joined = jnp.zeros((128, 256), F32)
            for h in range(4):
                joined = jnp.where(heads[h], mixed[128 * h : 128 * h + 128], joined)
            base = jnp.concatenate([ys[k, t, pl.ds(at, 32)] for t in range(4)], axis=0)
            done = (base.astype(F32) + mm(joined.astype(BF), wout_ref[...])).astype(BF)
            for t in range(4):
                osb[t, pl.ds(at, 32)] = done[32 * t : 32 * t + 32]
            return carry

        lax.fori_loop(0, 4, tile, 0)
        back = mm(hot_u[...], osb[...].reshape(512, 256)).astype(BF)
        rb[k] = back.reshape(32, 16, 256)
        spread(lambda peer: rb.at[k, peer], lambda mine: orv.at[mine, k], 6 + k)
        orv[me, k] = rb[k, me]

    above, below, across = (z + 1) & 3, (z + 3) & 3, (z + 2) & 3
    core_copy.wait()
    for part in range(4):
        gf[core, part] = gf[core, part] + r1[part].astype(F32)
        s1b[part] = gf[core, part].astype(BF)
    low, high = pl.ds(0, 8), pl.ds(8, 8)
    z_first = [
        reduce_copy(s1b.at[across, low], zu.at[0], 1, {"dp": above}),
        reduce_copy(s1b.at[across, high], zd.at[0], 2, {"dp": below}),
        reduce_copy(s1b.at[above, high], zu.at[1], 3, {"dp": above}),
        reduce_copy(s1b.at[below, low], zd.at[1], 4, {"dp": below}),
    ]
    for copy in z_first:
        copy.start()
    cell(0)
    z_first[0].wait()
    z_first[1].wait()
    s1b[above, 0:8] = (gf[core, above, 0:8] + zu[0].astype(F32)).astype(BF)
    s1b[below, 8:16] = (gf[core, below, 8:16] + zd[0].astype(F32)).astype(BF)
    z_second = [
        reduce_copy(s1b.at[above, low], zu.at[2], 5, {"dp": above}),
        reduce_copy(s1b.at[below, high], zd.at[2], 6, {"dp": below}),
    ]
    for copy in z_second:
        copy.start()
    cell(1)
    for copy in z_first[2:] + z_second:
        copy.wait()
    acc2[0:8] = gf[core, z, 0:8] + zu[2].astype(F32) + zd[1].astype(F32)
    acc2[8:16] = gf[core, z, 8:16] + zu[1].astype(F32) + zd[2].astype(F32)
    s2b[...] = acc2[...].astype(BF)
    y_copies = []
    for d in (1, 2, 3):
        yp = (chip_y + d) & 3
        y_copies.append(
            reduce_copy(s2b.at[pl.ds(yp * 4, 4)], r3.at[d - 1], 6 + d, {"ctx": (yp * 4 + chip_x) * 2 + core})
        )
    for copy in y_copies:
        copy.start()
    cell(2)
    for copy in y_copies:
        copy.wait()
    acc3[...] = acc2[pl.ds(chip_y * 4, 4)] + r3[0].astype(F32) + r3[1].astype(F32) + r3[2].astype(F32)
    s3b[...] = acc3[...].astype(BF)
    x_copies = []
    for d in (1, 2, 3):
        xq = (chip_x + d) & 3
        x_copies.append(
            reduce_copy(s3b.at[xq], r4.at[d - 1], 9 + d, {"ctx": (chip_y * 4 + xq) * 2 + core})
        )
    for copy in x_copies:
        copy.start()
    cell(3)
    for copy in x_copies:
        copy.wait()
    s4[...] = acc3[chip_x] + r4[0].astype(F32) + r4[1].astype(F32) + r4[2].astype(F32)
    end_copies = [
        reduce_copy(s4, r5.at[z], 12 + d, {"dp": (z + d) & 3}) for d in (1, 2, 3)
    ]
    for copy in end_copies:
        copy.start()
    r5[z] = s4[...]

    for k in range(4):
        landed(orv.at[pl.ds(0, DEV - 1), k], 6 + k)
    loads[10].wait()
    po = po_ref[...]
    for r in range(8):
        rows = orv[4 * r : 4 * r + 4].reshape(256, 256)
        moved = mm(po, rows).astype(BF)
        for s in range(4):
            for t in range(4):
                at = (s * 4 + t) * 16
                out_ref[s, t, 16 * r : 16 * r + 16] = moved[at : at + 16]
    for copy in end_copies:
        copy.wait()
    for part in range(4):
        cg_ref[27 * part : 27 * part + 27] = r5[part, 0:27]

    left(t1r.at[:, pl.ds(0, DEV - 1)], 0)
    left(t2s.at[:, pl.ds(0, DEV - 1)], 1)
    for t in range(4):
        left(cs.at[pl.ds(0, DEV - 1), t], 2 + t)
    for k in range(4):
        left(rb.at[k, pl.ds(0, DEV - 1)], 6 + k)


def per_device(pictures, slots, counts, scaling, taps, triple, final, upstream):
    vm = lambda shape, kind: pltpu.VMEM(shape, kind)
    scratch = [
        vm((4, 8, 8, 16, 128), BF),
        vm((384, 256), BF),
        vm((4, 4, 128, 256), BF),
        vm((256, 256), BF),
        vm((3456, 256), BF),
        vm((128, 512), BF),
        vm((256, 128), BF),
        vm((256, 768), BF),
        vm((256, 256), BF),
        vm((256, 256), BF),
        vm((256, 256), BF),
        vm((8, 10, 6, 16, 128), BF),
        vm((2, 10, 6, 16, 128), BF),
        vm((2048, 3456), BF),
        vm((2, 32, 16, 128), BF),
        vm((2, 32, 16, 128), BF),
        vm((2, 32, 16, 128), BF),
        vm((32, 4, 16, 256), BF),
        vm((32, 4, 16, 256), BF),
        vm((256, 2048), BF),
        vm((256, 2304), F32),
        vm((3464, 256), F32),
        vm((2, 4, 16, 32, 256), F32),
        vm((4, 16, 32, 256), BF),
        vm((4, 16, 32, 256), BF),
        vm((4, 16, 32, 256), BF),
        vm((3, 8, 32, 256), BF),
        vm((3, 8, 32, 256), BF),
        vm((16, 32, 256), F32),
        vm((16, 32, 256), BF),
        vm((3, 4, 32, 256), BF),
        vm((4, 32, 256), BF),
        vm((4, 32, 256), F32),
        vm((3, 32, 256), BF),
        vm((32, 256), F32),
        vm((4, 32, 256), F32),
        vm((512, 512), BF),
        vm((512, 512), BF),
        vm((512, 512), BF),
        vm((4, 128, 192), BF),
        vm((4, 4, 128, 256), BF),
        vm((4, 128, 256), BF),
        vm((4, 144, 256), BF),
        vm((4, 144, 256), BF),
        vm((4, 128, 256), BF),
        vm((4, 32, 16, 256), BF),
        vm((32, 4, 16, 256), BF),
        pltpu.SemaphoreType.DMA((10,)),
        pltpu.SemaphoreType.DMA((10,)),
        pltpu.SemaphoreType.DMA((16,)),
        pltpu.SemaphoreType.DMA((16,)),
        pltpu.SemaphoreType.DMA((11,)),
    ]
    v = pl.BlockSpec(memory_space=pltpu.VMEM)
    s = pl.BlockSpec(memory_space=pltpu.SMEM)
    h = pl.BlockSpec(memory_space=pl.ANY)
    latents, conv_grad = pl.pallas_call(
        section_kernel,
        out_shape=(
            jax.ShapeDtypeStruct((4, 4, 128, 256), BF),
            jax.ShapeDtypeStruct((108, 256), F32),
        ),
        in_specs=[h, h, h, h, h, v, s, s, h, h, h, h, h, h],
        out_specs=(v, v),
        scratch_shapes=scratch,
        compiler_params=pltpu.CompilerParams(
            collective_id=0, has_side_effects=True, vmem_limit_bytes=62 * 1024 * 1024
        ),
    )(
        pictures[0], taps, triple, final, upstream[0], slots.reshape(1, 128), counts, scaling,
        frame_rows(), gradient_rows(), result_rows(), column_shifts(), slot_expand(), head_sums(),
    )
    return latents[None], conv_grad


def solution(mesh):
    placed = (
        P("dp", "ctx", None, None, None, None),
        P(), P(), P(), P(), P(), P(),
        P("dp", "ctx", None, None, None),
    )
    return jax.shard_map(
        per_device,
        mesh=mesh,
        in_specs=placed,
        out_specs=(P("dp", "ctx", None, None, None), P("ctx", None)),
        check_vma=False,
    )
```

```python
import jax
import jax.numpy as jnp
import numpy as np
from jax import lax
from jax.experimental import pallas as pl
from jax.experimental.pallas import tpu as pltpu
from jax.sharding import PartitionSpec as P

BF = jnp.bfloat16
F32 = jnp.float32
MESH = pl.DeviceIdType.MESH
DEV = 32
UNROLL = 4
LOG2E = 1.4426950408889634


def one_hot_rows(rows, cols, pairs):
    table = np.zeros((rows, cols), np.float32)
    for row, col in pairs:
        table[row, col] = 1.0
    return jnp.asarray(table, BF)


def frame_rows():
    pairs = []
    for r in range(4):
        for qp in range(-1, 5):
            for k in range(4):
                for s in range(4):
                    q = qp + 4 * k
                    if 0 <= q < 16:
                        pairs.append((((r * 6 + qp + 1) * 4 + k) * 4 + s, (r * 4 + s) * 16 + q))
    return one_hot_rows(384, 256, pairs)


def gradient_rows():
    pairs = []
    for r in range(4):
        for qp in range(4):
            for k in range(4):
                for s in range(4):
                    pairs.append((((r * 4 + qp) * 4 + k) * 4 + s, (r * 4 + s) * 16 + qp + 4 * k))
    return one_hot_rows(256, 256, pairs)


def result_rows():
    pairs = []
    for qp in range(4):
        for k in range(4):
            for t in range(4):
                for s in range(4):
                    pairs.append(((s * 4 + t) * 16 + qp + 4 * k, ((qp * 4 + k) * 4 + t) * 4 + s))
    return one_hot_rows(256, 256, pairs)


def column_shifts():
    pairs = []
    for r in range(8):
        for k in range(4):
            for s in range(4):
                if k < 3:
                    pairs.append(((r * 4 + k) * 4 + s, (r * 4 + k + 1) * 4 + s))
                if k > 0:
                    pairs.append((128 + (r * 4 + k) * 4 + s, (r * 4 + k - 1) * 4 + s))
    return one_hot_rows(256, 128, pairs)


def slot_expand():
    pairs = []
    for e in range(32):
        for k in range(4):
            for s in range(4):
                pairs.append((4 * e + s, (e * 4 + k) * 4 + s))
    return one_hot_rows(128, 512, pairs)


def head_sums():
    table = np.kron(np.eye(4), np.ones((64, 64)))
    return jnp.asarray(table, BF)


def mm(a, b):
    return jnp.dot(a, b, preferred_element_type=F32)


def section_kernel(
    x_hbm, w_hbm, wqkv_hbm, wout_hbm, ug_hbm, sa_ref, cnt_ref, scale_ref,
    px_hbm, pg_hbm, sh_hbm, ex_hbm, hs_hbm,
    back_ref, rows_ref,
    x_ref, px_ref, ug_ref, pg_ref, w_ref, ex_ref, sh_ref, wqkv_ref, hs_ref, wout_ref,
    xp, xt, pat, t1r, t2s, t2r, cs, cr, gt, dwt, dw, gf, gbs, r1, s1b, r2, acc2, s2b, r3, s4,
    hot_t, hot_s, hot_u, mask, ys, qs, ks, vs, osb, rb,
    send_sem, recv_sem, red_send, red_recv, in_sem,
):
    z = lax.axis_index("dp")
    me = lax.axis_index("ctx")
    core = me & 1
    chip_x = (me >> 1) & 3
    chip_y = me >> 3

    loads = [
        pltpu.make_async_copy(source, target, in_sem.at[n])
        for n, (source, target) in enumerate((
            (x_hbm, x_ref), (px_hbm, px_ref), (ug_hbm, ug_ref), (pg_hbm, pg_ref), (w_hbm, w_ref), (ex_hbm, ex_ref),
            (sh_hbm, sh_ref), (wqkv_hbm, wqkv_ref), (hs_hbm, hs_ref), (wout_hbm, wout_ref),
        ))
    ]
    for load in loads:
        load.start()

    barrier = pltpu.get_barrier_semaphore()

    def greet(step, carry):
        peer = (me + step) & (DEV - 1)
        pl.semaphore_signal(barrier, inc=1, device_id={"ctx": peer}, device_id_type=MESH)
        return carry

    lax.fori_loop(1, DEV, greet, 0)
    for dz in range(1, 4):
        pl.semaphore_signal(barrier, inc=1, device_id={"dp": (z + dz) & 3}, device_id_type=MESH)

    def spread(source, target, phase):
        for step in range(1, DEV):
            peer = (me + step) & (DEV - 1)
            pltpu.make_async_remote_copy(
                src_ref=source(peer), dst_ref=target(me), send_sem=send_sem.at[phase],
                recv_sem=recv_sem.at[phase], device_id={"ctx": peer}, device_id_type=MESH,
            ).start()

    def landed(view, phase):
        pltpu.make_async_copy(view, view, recv_sem.at[phase]).wait()

    def left(view, phase):
        pltpu.make_async_copy(view, view, send_sem.at[phase]).wait()

    zero_rows = jnp.zeros((8, 6, 16, 128), BF)
    xp[:, 0] = zero_rows
    xp[:, 9] = zero_rows
    xt[:, 0] = zero_rows[:2]
    xt[:, 9] = zero_rows[:2]
    loads[0].wait()
    loads[1].wait()
    px = px_ref[...]
    for pair in (3, 0, 1, 2):
        for g in range(2):
            rows = []
            for r in range(4 * g, 4 * g + 4):
                for s in range(4):
                    rows.append(
                        jnp.concatenate([x_ref[s, 2 * pair, r], x_ref[s, 2 * pair + 1, r]], axis=1)
                    )
            moved = mm(px, jnp.concatenate(rows, axis=0)).astype(BF)
            for f in range(2):
                xp[2 * pair + f, 1 + 4 * g : 5 + 4 * g] = moved[:, 128 * f : 128 * f + 128].reshape(4, 6, 16, 128)

    def taps(t, tail, kts):
        for kt in kts:
            for kh in range(3):
                for kw in range(3):
                    tap = (kt * 3 + kh) * 3 + kw
                    if tail:
                        tile = xt[kt, kh : kh + 8, kw : kw + 4]
                    else:
                        tile = xp[2 * t - 2 + kt, kh : kh + 8, kw : kw + 4]
                    pat[pl.ds(512 * t, 512), 128 * tap : 128 * tap + 128] = tile.reshape(512, 128)

    def convolve(t):
        for half in range(2):
            rows = pat[pl.ds(512 * t + 256 * half, 256), :]
            cs[pl.ds(16 * half, 16), t] = mm(rows, w_ref[...]).astype(BF).reshape(16, 16, 256)
        cr[me, t] = cs[me, t]

    def send_frame(t):
        spread(lambda peer: cs.at[peer, t], lambda mine: cr.at[mine, t], 2 + t)

    loads[4].wait()
    taps(1, False, (0, 1, 2))
    convolve(1)
    loads[2].wait()
    loads[3].wait()
    pg = pg_ref[...]
    for t in range(4):
        for g in range(2):
            rows = []
            for r in range(4 * g, 4 * g + 4):
                for s in range(4):
                    rows.append(ug_ref[s, t, 16 * r : 16 * r + 16])
            moved = mm(pg, jnp.concatenate(rows, axis=0))
            at = (2 * t + g) * 256
            gt[:, at : at + 256] = jnp.transpose(moved).astype(BF)
    taps(2, False, (0, 1, 2))
    convolve(2)
    pl.semaphore_wait(barrier, DEV - 1 + 3)

    my_r, my_q = me >> 2, me & 3
    spread(
        lambda peer: xp.at[pl.ds(6, 2), (peer >> 2) + 1, (peer & 3) + 1],
        lambda mine: t1r.at[:, mine],
        0,
    )
    send_frame(1)
    t1r[:, me] = xp[6:8, my_r + 1, my_q + 1]

    taps(3, False, (0, 1, 2))
    convolve(3)
    taps(0, False, (2,))

    loads[5].wait()
    sa = sa_ref[...].astype(F32)
    opening = jnp.zeros((1, 128), jnp.bool_)
    first = jnp.int32(0)
    for n in range(16):
        opening = opening | (sa == first.astype(F32))
        first = first + cnt_ref[n]
    wanted = jnp.where(opening, -1000.0, sa * 4.0 - 4.0)
    codes = jnp.concatenate([sa * 4.0, wanted, jnp.zeros((14, 128), F32)], axis=0).astype(BF)
    wide = mm(codes, ex_ref[...])
    lane = lax.broadcasted_iota(jnp.int32, (1, 512), 1)
    kpat = ((lane >> 2) & 3).astype(F32)
    vrow = wide[0:1] + kpat
    wrow = wide[1:2] + kpat
    vcol = jnp.transpose(jnp.broadcast_to(vrow, (128, 512)))
    wcol = jnp.transpose(jnp.broadcast_to(wrow, (128, 512)))
    lane128 = lax.broadcasted_iota(jnp.int32, (1, 128), 1).astype(F32)
    for j in range(4):
        cols = slice(128 * j, 128 * j + 128)
        hot_t[:, cols] = jnp.where(wcol == vrow[:, cols], 1.0, 0.0).astype(BF)
        hot_u[:, cols] = jnp.where(vcol == lane128 * 4.0 + j, 1.0, 0.0).astype(BF)
        ids = lax.broadcasted_iota(jnp.int32, (128, 1), 0).astype(F32) * 4.0 + j
        hot_s[cols, :] = jnp.where(ids == vrow, 1.0, 0.0).astype(BF)

    def see(a, carry):
        row = lax.broadcasted_iota(jnp.int32, (128, 192), 0)
        col = lax.broadcasted_iota(jnp.int32, (128, 192), 1)
        span = 32 * a + (row & 31)
        when = span * 4 + (row >> 5)
        col_t = (col >= 48).astype(jnp.int32) + (col >= 96).astype(jnp.int32) + (col >= 144).astype(jnp.int32)
        other = 32 * a - 16 + col - 48 * col_t
        start = jnp.zeros((128, 192), jnp.int32)
        total = jnp.int32(0)
        for n in range(15):
            total = total + cnt_ref[n]
            start = jnp.where(span >= total, total, start)
        seen = (other >= start) & (other * 4 + col_t <= when)
        mask[a] = jnp.where(seen, 1.0, 0.0).astype(BF)
        return carry

    lax.fori_loop(0, 4, see, 0)
    ks[:, :, 0:16] = jnp.zeros((4, 4, 16, 256), BF)
    vs[:, :, :, 0:16, 0:128] = jnp.zeros((2, 4, 4, 16, 128), BF)
    vs[:, :, :, :, 128:256] = jnp.ones((2, 4, 4, 144, 128), BF)


    def grad_last(n, carry):
        at = pl.multiple_of(2304 + n * 256, 256)
        dw[pl.ds(at, 256), :] = jnp.transpose(mm(gt[...], pat[:, pl.ds(at, 256)]))
        return carry

    lax.fori_loop(0, 4, grad_last, 0)
    dw[3328:3456, :] = jnp.transpose(mm(gt[...], pat[:, 3328:3456]))
    dw[3456:3464, :] = jnp.zeros((8, 256), F32)

    partner = me + 1 - 2 * core

    def reduce_copy(source, target, index, where):
        return pltpu.make_async_remote_copy(
            src_ref=source, dst_ref=target, send_sem=red_send.at[index],
            recv_sem=red_recv.at[index], device_id=where, device_id_type=MESH,
        )

    def regroup(g, carry):
        block = dw[pl.ds(pl.multiple_of(216 * g, 8), 224), :]
        for j in range(8):
            gf[j // 4, j % 4, g] = block[27 * j : 27 * j + 32]
        return carry

    def to_partner(first, last, index):
        lax.fori_loop(first, last, regroup, 0)
        for part in range(4):
            gbs[part, first:last] = gf[1 - core, part, first:last].astype(BF)
        span = pl.ds(first, last - first)
        copies = [
            reduce_copy(gbs.at[part, span], r1.at[part, span], index, {"ctx": partner}) for part in range(4)
        ]
        for copy in copies:
            copy.start()

    def to_planes(first, last, index):
        span = pl.ds(first, last - first)
        pltpu.make_async_copy(r1.at[:, span], r1.at[:, span], red_recv.at[index]).wait()
        for part in range(4):
            whole = gf[core, part, first:last] + r1[part, first:last].astype(F32)
            gf[core, part, first:last] = whole
            s1b[part, first:last] = whole.astype(BF)
        copies = [
            reduce_copy(s1b.at[(z + d) & 3, span], r2.at[d - 1, span], index + d, {"dp": (z + d) & 3}) for d in (1, 3, 2)
        ]
        for copy in copies:
            copy.start()
        return copies

    to_partner(11, 16, 0)

    landed(t1r.at[:, pl.ds(0, DEV - 1)], 0)
    both = jnp.concatenate([t1r[0].reshape(512, 128), t1r[1].reshape(512, 128)], axis=1)
    moved = mm(hot_t[...], both).astype(BF)
    t2s[0] = moved[:, :128].reshape(32, 16, 128)
    t2s[1] = moved[:, 128:].reshape(32, 16, 128)
    spread(lambda peer: t2s.at[:, peer], lambda mine: t2r.at[:, mine], 1)
    t2r[:, me] = t2s[:, me]

    def grad_main(n, carry):
        at = pl.multiple_of(n * 256, 256)
        dwt[:, pl.ds(at, 256)] = mm(gt[:, 512:2048], pat[512:2048, pl.ds(at, 256)])
        return carry

    lax.fori_loop(0, 3, grad_main, 0)
    send_frame(2)
    send_frame(3)
    lax.fori_loop(3, 9, grad_main, 0)

    for load in loads[7:10]:
        load.wait()
    lanes = lax.broadcasted_iota(jnp.int32, (1, 256), 1)
    heads = [(lanes >> 6) == h for h in range(4)]
    left_half = lax.broadcasted_iota(jnp.int32, (1, 128), 1) < 64
    scale = jnp.zeros((1, 256), F32)
    for h in range(4):
        scale = jnp.where(heads[h], scale_ref[h] * LOG2E, scale)

    def stream_rows(t):
        landed(cr.at[pl.ds(0, DEV - 1), t], 2 + t)
        rows = mm(hot_s[...], cr[:, t].reshape(512, 256)).astype(BF)
        wide = rows.astype(F32)
        mean = jnp.mean(wide * wide, axis=1, keepdims=True)
        normed = (wide * lax.rsqrt(mean + 1e-6)).astype(BF)
        query = mm(normed, wqkv_ref[:, 0:256])
        sums = mm((query * query).astype(BF), hs_ref[...])
        query = (query * (lax.rsqrt(sums + 1e-6) * scale)).astype(BF)
        key = mm(normed, wqkv_ref[:, 256:512])
        sums = mm((key * key).astype(BF), hs_ref[...])
        key = (key * lax.rsqrt(sums + 1e-6)).astype(BF)
        value = mm(normed, wqkv_ref[:, 512:768]).astype(BF)
        for k in range(4):
            mine = slice(128 * k, 128 * k + 128)
            ys[k, t] = rows[mine]
            qs[k, t] = query[mine]
            ks[k, t, 16:144] = key[mine]
            for p in range(2):
                vs[p, k, t, 16:144, 0:128] = value[mine, 128 * p : 128 * p + 128]

    stream_rows(1)
    z_copies = to_planes(11, 16, 0)
    landed(t2r.at[:, pl.ds(0, DEV - 1)], 1)
    loads[6].wait()
    for f in range(2):
        tiles = t2r[f].reshape(8, 4, 16, 128)
        xt[f, 1:9, 1:5] = tiles
        up = mm(sh_ref[0:128], tiles[:, 0].reshape(128, 128)).astype(BF)
        down = mm(sh_ref[128:256], tiles[:, 3].reshape(128, 128)).astype(BF)
        xt[f, 1:9, 5] = up.reshape(8, 16, 128)
        xt[f, 1:9, 0] = down.reshape(8, 16, 128)
    taps(0, True, (0, 1))
    convolve(0)
    send_frame(0)

    def grad_tail(n, carry):
        at = pl.multiple_of(n * 256, 256)
        part = dwt[:, pl.ds(at, 256)] + mm(gt[:, 0:512], pat[0:512, pl.ds(at, 256)])
        dw[pl.ds(at, 256), :] = jnp.transpose(part)
        return carry

    lax.fori_loop(0, 9, grad_tail, 0, unroll=3)
    to_partner(0, 11, 4)


    stream_rows(2)
    stream_rows(3)
    def cell(k):
        def tile(a, carry):
            at = pl.multiple_of(32 * a, 32)
            see_a = jnp.concatenate([mask[a]] * 2, axis=0)
            joined = []
            for p in range(2):
                pair = slice(128 * p, 128 * p + 128)
                qa = jnp.concatenate([qs[k, t, pl.ds(at, 32), pair] for t in range(4)], axis=0)
                zero = jnp.zeros_like(qa)
                stacked = jnp.concatenate([jnp.where(left_half, qa, zero), jnp.where(left_half, zero, qa)], axis=0)
                keys = jnp.concatenate([ks[k, t, pl.ds(at, 48), pair] for t in range(4)], axis=0)
                vals = jnp.concatenate([vs[p, k, t, pl.ds(at, 48)] for t in range(4)], axis=0)
                scores = lax.dot_general(
                    stacked, keys, (((1,), (1,)), ((), ())), preferred_element_type=F32
                )
                weights = jnp.exp2(scores).astype(BF) * see_a
                both = mm(weights, vals)
                above_line = jnp.where(left_half, both[0:128, 0:128], both[128:256, 0:128])
                below_line = jnp.where(left_half, both[0:128, 128:256], both[128:256, 128:256])
                joined.append((above_line / below_line).astype(BF))
            joined = jnp.concatenate(joined, axis=1)
            base = jnp.concatenate([ys[k, t, pl.ds(at, 32)] for t in range(4)], axis=0)
            done = (base.astype(F32) + mm(joined, wout_ref[...])).astype(BF)
            for t in range(4):
                osb[t, pl.ds(at, 32)] = done[32 * t : 32 * t + 32]
            return carry

        lax.fori_loop(0, 4, tile, 0, unroll=UNROLL)

    def ship(k):
        back = mm(hot_u[...], osb[...].reshape(512, 256)).astype(BF)
        rb[k] = back.reshape(32, 16, 256)
        spread(lambda peer: rb.at[k, peer], lambda mine: back_ref.at[mine, k], 6 + k)
        back_ref[me, k] = rb[k, me]

    z_copies += to_planes(0, 11, 4)
    stream_rows(0)
    for k in range(3):
        cell(k)
        ship(k)
    cell(3)

    for copy in z_copies:
        copy.wait()
    acc2[...] = gf[core, z] + r2[0].astype(F32) + r2[1].astype(F32) + r2[2].astype(F32)
    s2b[...] = acc2[...].astype(BF)
    chip = me >> 1
    plane_copies = []
    for d in range(1, 16):
        other = (chip + d) & 15
        plane_copies.append(reduce_copy(s2b.at[other], r3.at[d - 1], 8, {"ctx": other * 2 + core}))
    for copy in plane_copies:
        copy.start()
    ship(3)

    pltpu.make_async_copy(r3, r3, red_recv.at[8]).wait()
    total = acc2[chip]
    for d in range(15):
        total = total + r3[d].astype(F32)
    s4[...] = total
    end_copies = [
        reduce_copy(s4, rows_ref.at[z], 8 + d, {"dp": (z + d) & 3}) for d in (1, 2, 3)
    ]
    for copy in end_copies:
        copy.start()
    rows_ref[z] = s4[...]
    for k in range(4):
        landed(back_ref.at[pl.ds(0, DEV - 1), k], 6 + k)
    left(t1r.at[:, pl.ds(0, DEV - 1)], 0)
    left(t2s.at[:, pl.ds(0, DEV - 1)], 1)
    for t in range(4):
        left(cs.at[pl.ds(0, DEV - 1), t], 2 + t)
    for k in range(4):
        left(rb.at[k, pl.ds(0, DEV - 1)], 6 + k)
    pltpu.make_async_copy(r3, r3, red_send.at[8]).wait()
    for span, index in ((pl.ds(11, 5), 0), (pl.ds(0, 11), 4)):
        pltpu.make_async_copy(gbs.at[:, span], gbs.at[:, span], red_send.at[index]).wait()
    for copy in end_copies:
        copy.wait()


def place_kernel(back_ref, rows_ref, po_ref, out_ref, cg_ref):
    for r in range(8):
        moved = mm(po_ref[...], back_ref[4 * r : 4 * r + 4].reshape(256, 256)).astype(BF)
        for s in range(4):
            for t in range(4):
                at = (s * 4 + t) * 16
                out_ref[s, t, 16 * r : 16 * r + 16] = moved[at : at + 16]
    for part in range(4):
        cg_ref[27 * part : 27 * part + 27] = rows_ref[part, 0:27]


def per_device(pictures, slots, counts, scaling, taps, triple, final, upstream):
    vm = lambda shape, kind: pltpu.VMEM(shape, kind)
    scratch = [
        vm((4, 8, 8, 16, 128), BF),
        vm((384, 256), BF),
        vm((4, 4, 128, 256), BF),
        vm((256, 256), BF),
        vm((3456, 256), BF),
        vm((128, 512), BF),
        vm((256, 128), BF),
        vm((256, 768), BF),
        vm((256, 256), BF),
        vm((256, 256), BF),
        vm((8, 10, 6, 16, 128), BF),
        vm((2, 10, 6, 16, 128), BF),
        vm((2048, 3456), BF),
        vm((2, 32, 16, 128), BF),
        vm((2, 32, 16, 128), BF),
        vm((2, 32, 16, 128), BF),
        vm((32, 4, 16, 256), BF),
        vm((32, 4, 16, 256), BF),
        vm((256, 2048), BF),
        vm((256, 2304), F32),
        vm((3464, 256), F32),
        vm((2, 4, 16, 32, 256), F32),
        vm((4, 16, 32, 256), BF),
        vm((4, 16, 32, 256), BF),
        vm((4, 16, 32, 256), BF),
        vm((3, 16, 32, 256), BF),
        vm((16, 32, 256), F32),
        vm((16, 32, 256), BF),
        vm((15, 32, 256), BF),
        vm((32, 256), F32),
        vm((512, 512), BF),
        vm((512, 512), BF),
        vm((512, 512), BF),
        vm((4, 128, 192), BF),
        vm((4, 4, 128, 256), BF),
        vm((4, 4, 128, 256), BF),
        vm((4, 4, 144, 256), BF),
        vm((2, 4, 4, 144, 256), BF),
        vm((4, 128, 256), BF),
        vm((4, 32, 16, 256), BF),
        pltpu.SemaphoreType.DMA((10,)),
        pltpu.SemaphoreType.DMA((10,)),
        pltpu.SemaphoreType.DMA((12,)),
        pltpu.SemaphoreType.DMA((12,)),
        pltpu.SemaphoreType.DMA((10,)),
    ]
    v = pl.BlockSpec(memory_space=pltpu.VMEM)
    s = pl.BlockSpec(memory_space=pltpu.SMEM)
    h = pl.BlockSpec(memory_space=pl.ANY)
    back, rows = pl.pallas_call(
        section_kernel,
        out_shape=(
            jax.ShapeDtypeStruct((32, 4, 16, 256), BF),
            jax.ShapeDtypeStruct((4, 32, 256), F32),
        ),
        in_specs=[h, h, h, h, h, v, s, s, h, h, h, h, h],
        out_specs=(v, v),
        scratch_shapes=scratch,
        compiler_params=pltpu.CompilerParams(
            collective_id=0, has_side_effects=True, vmem_limit_bytes=62 * 1024 * 1024
        ),
    )(
        pictures[0], taps, triple, final, upstream[0], slots.reshape(1, 128), counts, scaling,
        frame_rows(), gradient_rows(), column_shifts(), slot_expand(), head_sums(),
    )
    latents, conv_grad = pl.pallas_call(
        place_kernel,
        out_shape=(
            jax.ShapeDtypeStruct((4, 4, 128, 256), BF),
            jax.ShapeDtypeStruct((108, 256), F32),
        ),
        in_specs=[v, v, v],
        out_specs=(v, v),
    )(back, rows, result_rows())
    return latents[None], conv_grad


def solution(mesh):
    placed = (
        P("dp", "ctx", None, None, None, None),
        P(), P(), P(), P(), P(), P(),
        P("dp", "ctx", None, None, None),
    )
    return jax.shard_map(
        per_device,
        mesh=mesh,
        in_specs=placed,
        out_specs=(P("dp", "ctx", None, None, None), P("ctx", None)),
        check_vma=False,
    )
```

```python
import jax
import jax.numpy as jnp
import numpy as np
from jax import lax
from jax.experimental import pallas as pl
from jax.experimental.pallas import tpu as pltpu
from jax.sharding import PartitionSpec as P

BF = jnp.bfloat16
F32 = jnp.float32
MESH = pl.DeviceIdType.MESH
DEV = 32
UNROLL = 4
LOG2E = 1.4426950408889634


def one_hot_rows(rows, cols, pairs):
    table = np.zeros((rows, cols), np.float32)
    for row, col in pairs:
        table[row, col] = 1.0
    return jnp.asarray(table, BF)


def frame_rows():
    pairs = []
    for r in range(4):
        for qp in range(-1, 5):
            for k in range(4):
                for s in range(4):
                    q = qp + 4 * k
                    if 0 <= q < 16:
                        pairs.append((((r * 6 + qp + 1) * 4 + k) * 4 + s, (r * 4 + s) * 16 + q))
    return one_hot_rows(384, 256, pairs)


def gradient_rows():
    pairs = []
    for r in range(4):
        for qp in range(4):
            for k in range(4):
                for s in range(4):
                    pairs.append((((r * 4 + qp) * 4 + k) * 4 + s, (r * 4 + s) * 16 + qp + 4 * k))
    return one_hot_rows(256, 256, pairs)


def result_rows():
    pairs = []
    for qp in range(4):
        for k in range(4):
            for t in range(4):
                for s in range(4):
                    pairs.append(((s * 4 + t) * 16 + qp + 4 * k, ((qp * 4 + k) * 4 + t) * 4 + s))
    return one_hot_rows(256, 256, pairs)


def column_shifts():
    pairs = []
    for r in range(8):
        for k in range(4):
            for s in range(4):
                if k < 3:
                    pairs.append(((r * 4 + k) * 4 + s, (r * 4 + k + 1) * 4 + s))
                if k > 0:
                    pairs.append((128 + (r * 4 + k) * 4 + s, (r * 4 + k - 1) * 4 + s))
    return one_hot_rows(256, 128, pairs)


def slot_expand():
    pairs = []
    for e in range(32):
        for k in range(4):
            for s in range(4):
                pairs.append((4 * e + s, (e * 4 + k) * 4 + s))
    return one_hot_rows(128, 512, pairs)


def head_sums():
    table = np.kron(np.eye(4), np.ones((64, 64)))
    return jnp.asarray(table, BF)


def mm(a, b):
    return jnp.dot(a, b, preferred_element_type=F32)


def section_kernel(
    x_hbm, w_hbm, wqkv_hbm, wout_hbm, ug_hbm, sa_ref, cnt_ref, scale_ref,
    px_hbm, pg_hbm, sh_hbm, ex_hbm, hs_hbm,
    back_ref, rows_ref,
    x_ref, px_ref, ug_ref, pg_ref, w_ref, ex_ref, sh_ref, wqkv_ref, hs_ref, wout_ref,
    xp, xt, pat, t1r, t2s, t2r, cs, cr, gt, dwt, dw, gf, gbs, r1, s1b, r2, acc2, s2b, r3, s4,
    hot_t, hot_s, hot_u, mask, ys, qs, ks, vs, osb, rb,
    send_sem, recv_sem, red_send, red_recv, in_sem,
):
    z = lax.axis_index("dp")
    me = lax.axis_index("ctx")
    core = me & 1
    chip_x = (me >> 1) & 3
    chip_y = me >> 3

    loads = [
        pltpu.make_async_copy(source, target, in_sem.at[n])
        for n, (source, target) in enumerate((
            (x_hbm, x_ref), (px_hbm, px_ref), (ug_hbm, ug_ref), (pg_hbm, pg_ref), (w_hbm, w_ref), (ex_hbm, ex_ref),
            (sh_hbm, sh_ref), (wqkv_hbm, wqkv_ref), (hs_hbm, hs_ref), (wout_hbm, wout_ref),
        ))
    ]
    for load in loads[:2]:
        load.start()

    barrier = pltpu.get_barrier_semaphore()

    for step in range(1, DEV):
        peer = (me + step) & (DEV - 1)
        pl.semaphore_signal(barrier, inc=1, device_id={"ctx": peer}, device_id_type=MESH)
    for dz in range(1, 4):
        pl.semaphore_signal(barrier, inc=1, device_id={"dp": (z + dz) & 3}, device_id_type=MESH)
    for load in loads[2:]:
        load.start()

    def spread(source, target, phase):
        for step in range(1, DEV):
            peer = (me + step) & (DEV - 1)
            pltpu.make_async_remote_copy(
                src_ref=source(peer), dst_ref=target(me), send_sem=send_sem.at[phase],
                recv_sem=recv_sem.at[phase], device_id={"ctx": peer}, device_id_type=MESH,
            ).start()

    def landed(view, phase):
        pltpu.make_async_copy(view, view, recv_sem.at[phase]).wait()

    def left(view, phase):
        pltpu.make_async_copy(view, view, send_sem.at[phase]).wait()

    zero_rows = jnp.zeros((8, 6, 16, 128), BF)
    xp[:, 0] = zero_rows
    xp[:, 9] = zero_rows
    xt[:, 0] = zero_rows[:2]
    xt[:, 9] = zero_rows[:2]
    loads[0].wait()
    loads[1].wait()
    px = px_ref[...]
    def frames_in(pair):
        for g in range(2):
            rows = []
            for r in range(4 * g, 4 * g + 4):
                for s in range(4):
                    rows.append(
                        jnp.concatenate([x_ref[s, 2 * pair, r], x_ref[s, 2 * pair + 1, r]], axis=1)
                    )
            moved = mm(px, jnp.concatenate(rows, axis=0)).astype(BF)
            for f in range(2):
                xp[2 * pair + f, 1 + 4 * g : 5 + 4 * g] = moved[:, 128 * f : 128 * f + 128].reshape(4, 6, 16, 128)

    frames_in(3)
    pl.semaphore_wait(barrier, DEV - 1 + 3)
    my_r, my_q = me >> 2, me & 3
    spread(
        lambda peer: xp.at[pl.ds(6, 2), (peer >> 2) + 1, (peer & 3) + 1],
        lambda mine: t1r.at[:, mine],
        0,
    )
    t1r[:, me] = xp[6:8, my_r + 1, my_q + 1]
    for pair in (0, 1, 2):
        frames_in(pair)
    partner = me + 1 - 2 * core

    def reduce_copy(source, target, index, where):
        return pltpu.make_async_remote_copy(
            src_ref=source, dst_ref=target, send_sem=red_send.at[index],
            recv_sem=red_recv.at[index], device_id=where, device_id_type=MESH,
        )

    def regroup(g, carry):
        block = dw[pl.ds(pl.multiple_of(216 * g, 8), 224), :]
        for j in range(8):
            gf[j // 4, j % 4, g] = block[27 * j : 27 * j + 32]
        return carry

    def to_partner(first, last, index):
        lax.fori_loop(first, last, regroup, 0)
        for part in range(4):
            gbs[part, first:last] = gf[1 - core, part, first:last].astype(BF)
        span = pl.ds(first, last - first)
        copies = [
            reduce_copy(gbs.at[part, span], r1.at[part, span], index, {"ctx": partner}) for part in range(4)
        ]
        for copy in copies:
            copy.start()

    def to_planes(first, last, index):
        span = pl.ds(first, last - first)
        pltpu.make_async_copy(r1.at[:, span], r1.at[:, span], red_recv.at[index]).wait()
        for part in range(4):
            whole = gf[core, part, first:last] + r1[part, first:last].astype(F32)
            gf[core, part, first:last] = whole
            s1b[part, first:last] = whole.astype(BF)
        copies = [
            reduce_copy(s1b.at[(z + d) & 3, span], r2.at[d - 1, span], index + d, {"dp": (z + d) & 3}) for d in (1, 3, 2)
        ]
        for copy in copies:
            copy.start()
        return copies

    def taps(t, tail, kts):
        for kt in kts:
            for kh in range(3):
                for kw in range(3):
                    tap = (kt * 3 + kh) * 3 + kw
                    if tail:
                        tile = xt[kt, kh : kh + 8, kw : kw + 4]
                    else:
                        tile = xp[2 * t - 2 + kt, kh : kh + 8, kw : kw + 4]
                    pat[pl.ds(512 * t, 512), 128 * tap : 128 * tap + 128] = tile.reshape(512, 128)

    def convolve(t):
        for half in range(2):
            rows = pat[pl.ds(512 * t + 256 * half, 256), :]
            cs[pl.ds(16 * half, 16), t] = mm(rows, w_ref[...]).astype(BF).reshape(16, 16, 256)
        cr[me, t] = cs[me, t]

    def send_frame(t):
        spread(lambda peer: cs.at[peer, t], lambda mine: cr.at[mine, t], 2 + t)

    loads[4].wait()
    taps(1, False, (0, 1, 2))
    convolve(1)
    send_frame(1)
    loads[2].wait()
    loads[3].wait()
    pg = pg_ref[...]
    for t in range(4):
        for g in range(2):
            rows = []
            for r in range(4 * g, 4 * g + 4):
                for s in range(4):
                    rows.append(ug_ref[s, t, 16 * r : 16 * r + 16])
            moved = mm(pg, jnp.concatenate(rows, axis=0))
            at = (2 * t + g) * 256
            gt[:, at : at + 256] = jnp.transpose(moved).astype(BF)
    taps(2, False, (0, 1, 2))
    convolve(2)
    taps(3, False, (0, 1, 2))
    convolve(3)
    taps(0, False, (2,))

    loads[5].wait()
    sa = sa_ref[...].astype(F32)
    opening = jnp.zeros((1, 128), jnp.bool_)
    first = jnp.int32(0)
    for n in range(16):
        opening = opening | (sa == first.astype(F32))
        first = first + cnt_ref[n]
    wanted = jnp.where(opening, -1000.0, sa * 4.0 - 4.0)
    codes = jnp.concatenate([sa * 4.0, wanted, jnp.zeros((14, 128), F32)], axis=0).astype(BF)
    wide = mm(codes, ex_ref[...])
    lane = lax.broadcasted_iota(jnp.int32, (1, 512), 1)
    kpat = ((lane >> 2) & 3).astype(F32)
    vrow = wide[0:1] + kpat
    wrow = wide[1:2] + kpat
    vcol = jnp.transpose(jnp.broadcast_to(vrow, (128, 512)))
    wcol = jnp.transpose(jnp.broadcast_to(wrow, (128, 512)))
    lane128 = lax.broadcasted_iota(jnp.int32, (1, 128), 1).astype(F32)
    for j in range(4):
        cols = slice(128 * j, 128 * j + 128)
        hot_t[:, cols] = jnp.where(wcol == vrow[:, cols], 1.0, 0.0).astype(BF)
        hot_u[:, cols] = jnp.where(vcol == lane128 * 4.0 + j, 1.0, 0.0).astype(BF)
        ids = lax.broadcasted_iota(jnp.int32, (128, 1), 0).astype(F32) * 4.0 + j
        hot_s[cols, :] = jnp.where(ids == vrow, 1.0, 0.0).astype(BF)

    def see(a, carry):
        row = lax.broadcasted_iota(jnp.int32, (128, 192), 0)
        col = lax.broadcasted_iota(jnp.int32, (128, 192), 1)
        span = 32 * a + (row & 31)
        when = span * 4 + (row >> 5)
        col_t = (col >= 48).astype(jnp.int32) + (col >= 96).astype(jnp.int32) + (col >= 144).astype(jnp.int32)
        other = 32 * a - 16 + col - 48 * col_t
        start = jnp.zeros((128, 192), jnp.int32)
        total = jnp.int32(0)
        for n in range(15):
            total = total + cnt_ref[n]
            start = jnp.where(span >= total, total, start)
        seen = (other >= start) & (other * 4 + col_t <= when)
        mask[a] = jnp.where(seen, 1.0, 0.0).astype(BF)
        return carry

    lax.fori_loop(0, 4, see, 0)
    ks[:, :, 0:16] = jnp.zeros((4, 4, 16, 256), BF)
    vs[:, :, :, 0:16, 0:128] = jnp.zeros((2, 4, 4, 16, 128), BF)
    vs[:, :, :, :, 128:256] = jnp.ones((2, 4, 4, 144, 128), BF)


    landed(t1r.at[:, pl.ds(0, DEV - 1)], 0)
    both = jnp.concatenate([t1r[0].reshape(512, 128), t1r[1].reshape(512, 128)], axis=1)
    moved = mm(hot_t[...], both).astype(BF)
    t2s[0] = moved[:, :128].reshape(32, 16, 128)
    t2s[1] = moved[:, 128:].reshape(32, 16, 128)
    spread(lambda peer: t2s.at[:, peer], lambda mine: t2r.at[:, mine], 1)
    t2r[:, me] = t2s[:, me]
    send_frame(2)

    def grad_last(n, carry):
        at = pl.multiple_of(2304 + n * 256, 256)
        dw[pl.ds(at, 256), :] = jnp.transpose(mm(gt[...], pat[:, pl.ds(at, 256)]))
        return carry

    lax.fori_loop(0, 4, grad_last, 0)
    dw[3328:3456, :] = jnp.transpose(mm(gt[...], pat[:, 3328:3456]))
    dw[3456:3464, :] = jnp.zeros((8, 256), F32)

    to_partner(11, 16, 0)

    def grad_main(n, carry):
        at = pl.multiple_of(n * 256, 256)
        dwt[:, pl.ds(at, 256)] = mm(gt[:, 512:2048], pat[512:2048, pl.ds(at, 256)])
        return carry

    lax.fori_loop(0, 3, grad_main, 0)
    send_frame(3)
    lax.fori_loop(3, 9, grad_main, 0)

    for load in loads[7:10]:
        load.wait()
    lanes = lax.broadcasted_iota(jnp.int32, (1, 256), 1)
    heads = [(lanes >> 6) == h for h in range(4)]
    left_half = lax.broadcasted_iota(jnp.int32, (1, 128), 1) < 64
    scale = jnp.zeros((1, 256), F32)
    for h in range(4):
        scale = jnp.where(heads[h], scale_ref[h] * LOG2E, scale)

    def stream_rows(t):
        landed(cr.at[pl.ds(0, DEV - 1), t], 2 + t)
        rows = mm(hot_s[...], cr[:, t].reshape(512, 256)).astype(BF)
        wide = rows.astype(F32)
        mean = jnp.mean(wide * wide, axis=1, keepdims=True)
        normed = (wide * lax.rsqrt(mean + 1e-6)).astype(BF)
        query = mm(normed, wqkv_ref[:, 0:256])
        sums = mm((query * query).astype(BF), hs_ref[...])
        query = (query * (lax.rsqrt(sums + 1e-6) * scale)).astype(BF)
        key = mm(normed, wqkv_ref[:, 256:512])
        sums = mm((key * key).astype(BF), hs_ref[...])
        key = (key * lax.rsqrt(sums + 1e-6)).astype(BF)
        value = mm(normed, wqkv_ref[:, 512:768]).astype(BF)
        for k in range(4):
            mine = slice(128 * k, 128 * k + 128)
            ys[k, t] = rows[mine]
            qs[k, t] = query[mine]
            ks[k, t, 16:144] = key[mine]
            for p in range(2):
                vs[p, k, t, 16:144, 0:128] = value[mine, 128 * p : 128 * p + 128]

    z_copies = to_planes(11, 16, 0)
    landed(t2r.at[:, pl.ds(0, DEV - 1)], 1)
    loads[6].wait()
    for f in range(2):
        tiles = t2r[f].reshape(8, 4, 16, 128)
        xt[f, 1:9, 1:5] = tiles
        up = mm(sh_ref[0:128], tiles[:, 0].reshape(128, 128)).astype(BF)
        down = mm(sh_ref[128:256], tiles[:, 3].reshape(128, 128)).astype(BF)
        xt[f, 1:9, 5] = up.reshape(8, 16, 128)
        xt[f, 1:9, 0] = down.reshape(8, 16, 128)
    taps(0, True, (0, 1))
    convolve(0)
    send_frame(0)

    def grad_tail(n, carry):
        at = pl.multiple_of(n * 256, 256)
        part = dwt[:, pl.ds(at, 256)] + mm(gt[:, 0:512], pat[0:512, pl.ds(at, 256)])
        dw[pl.ds(at, 256), :] = jnp.transpose(part)
        return carry

    lax.fori_loop(0, 9, grad_tail, 0, unroll=3)
    to_partner(0, 11, 4)


    stream_rows(1)
    stream_rows(2)
    stream_rows(3)
    def cell(k):
        def tile(a, carry):
            at = pl.multiple_of(32 * a, 32)
            see_a = jnp.concatenate([mask[a]] * 2, axis=0)
            joined = []
            for p in range(2):
                pair = slice(128 * p, 128 * p + 128)
                qa = jnp.concatenate([qs[k, t, pl.ds(at, 32), pair] for t in range(4)], axis=0)
                zero = jnp.zeros_like(qa)
                stacked = jnp.concatenate([jnp.where(left_half, qa, zero), jnp.where(left_half, zero, qa)], axis=0)
                keys = jnp.concatenate([ks[k, t, pl.ds(at, 48), pair] for t in range(4)], axis=0)
                vals = jnp.concatenate([vs[p, k, t, pl.ds(at, 48)] for t in range(4)], axis=0)
                scores = lax.dot_general(
                    stacked, keys, (((1,), (1,)), ((), ())), preferred_element_type=F32
                )
                weights = jnp.exp2(scores).astype(BF) * see_a
                both = mm(weights, vals)
                above_line = jnp.where(left_half, both[0:128, 0:128], both[128:256, 0:128])
                below_line = jnp.where(left_half, both[0:128, 128:256], both[128:256, 128:256])
                joined.append((above_line / below_line).astype(BF))
            joined = jnp.concatenate(joined, axis=1)
            base = jnp.concatenate([ys[k, t, pl.ds(at, 32)] for t in range(4)], axis=0)
            done = (base.astype(F32) + mm(joined, wout_ref[...])).astype(BF)
            for t in range(4):
                osb[t, pl.ds(at, 32)] = done[32 * t : 32 * t + 32]
            return carry

        lax.fori_loop(0, 4, tile, 0, unroll=UNROLL)

    def ship(k):
        back = mm(hot_u[...], osb[...].reshape(512, 256)).astype(BF)
        rb[k] = back.reshape(32, 16, 256)
        spread(lambda peer: rb.at[k, peer], lambda mine: back_ref.at[mine, k], 6 + k)
        back_ref[me, k] = rb[k, me]

    z_copies += to_planes(0, 11, 4)
    stream_rows(0)
    cell(0)
    ship(0)
    cell(1)
    ship(1)
    cell(2)

    for copy in z_copies:
        copy.wait()
    acc2[...] = gf[core, z] + r2[0].astype(F32) + r2[1].astype(F32) + r2[2].astype(F32)
    s2b[...] = acc2[...].astype(BF)
    chip = me >> 1
    plane_copies = []
    for d in range(1, 16):
        other = (chip + d) & 15
        plane_copies.append(reduce_copy(s2b.at[other], r3.at[d - 1], 8, {"ctx": other * 2 + core}))
    for copy in plane_copies:
        copy.start()
    ship(2)
    cell(3)
    ship(3)

    pltpu.make_async_copy(r3, r3, red_recv.at[8]).wait()
    total = acc2[chip]
    for d in range(15):
        total = total + r3[d].astype(F32)
    s4[...] = total
    end_copies = [
        reduce_copy(s4, rows_ref.at[z], 8 + d, {"dp": (z + d) & 3}) for d in (1, 2, 3)
    ]
    for copy in end_copies:
        copy.start()
    rows_ref[z] = s4[...]
    for k in range(4):
        landed(back_ref.at[pl.ds(0, DEV - 1), k], 6 + k)
    left(t1r.at[:, pl.ds(0, DEV - 1)], 0)
    left(t2s.at[:, pl.ds(0, DEV - 1)], 1)
    for t in range(4):
        left(cs.at[pl.ds(0, DEV - 1), t], 2 + t)
    for k in range(4):
        left(rb.at[k, pl.ds(0, DEV - 1)], 6 + k)
    pltpu.make_async_copy(r3, r3, red_send.at[8]).wait()
    for span, index in ((pl.ds(11, 5), 0), (pl.ds(0, 11), 4)):
        pltpu.make_async_copy(gbs.at[:, span], gbs.at[:, span], red_send.at[index]).wait()
    for copy in end_copies:
        copy.wait()


def place_kernel(back_ref, rows_ref, po_ref, out_ref, cg_ref):
    for r in range(8):
        moved = mm(po_ref[...], back_ref[4 * r : 4 * r + 4].reshape(256, 256)).astype(BF)
        for s in range(4):
            for t in range(4):
                at = (s * 4 + t) * 16
                out_ref[s, t, 16 * r : 16 * r + 16] = moved[at : at + 16]
    for part in range(4):
        cg_ref[27 * part : 27 * part + 27] = rows_ref[part, 0:27]


def per_device(pictures, slots, counts, scaling, taps, triple, final, upstream):
    vm = lambda shape, kind: pltpu.VMEM(shape, kind)
    scratch = [
        vm((4, 8, 8, 16, 128), BF),
        vm((384, 256), BF),
        vm((4, 4, 128, 256), BF),
        vm((256, 256), BF),
        vm((3456, 256), BF),
        vm((128, 512), BF),
        vm((256, 128), BF),
        vm((256, 768), BF),
        vm((256, 256), BF),
        vm((256, 256), BF),
        vm((8, 10, 6, 16, 128), BF),
        vm((2, 10, 6, 16, 128), BF),
        vm((2048, 3456), BF),
        vm((2, 32, 16, 128), BF),
        vm((2, 32, 16, 128), BF),
        vm((2, 32, 16, 128), BF),
        vm((32, 4, 16, 256), BF),
        vm((32, 4, 16, 256), BF),
        vm((256, 2048), BF),
        vm((256, 2304), F32),
        vm((3464, 256), F32),
        vm((2, 4, 16, 32, 256), F32),
        vm((4, 16, 32, 256), BF),
        vm((4, 16, 32, 256), BF),
        vm((4, 16, 32, 256), BF),
        vm((3, 16, 32, 256), BF),
        vm((16, 32, 256), F32),
        vm((16, 32, 256), BF),
        vm((15, 32, 256), BF),
        vm((32, 256), F32),
        vm((512, 512), BF),
        vm((512, 512), BF),
        vm((512, 512), BF),
        vm((4, 128, 192), BF),
        vm((4, 4, 128, 256), BF),
        vm((4, 4, 128, 256), BF),
        vm((4, 4, 144, 256), BF),
        vm((2, 4, 4, 144, 256), BF),
        vm((4, 128, 256), BF),
        vm((4, 32, 16, 256), BF),
        pltpu.SemaphoreType.DMA((10,)),
        pltpu.SemaphoreType.DMA((10,)),
        pltpu.SemaphoreType.DMA((12,)),
        pltpu.SemaphoreType.DMA((12,)),
        pltpu.SemaphoreType.DMA((10,)),
    ]
    v = pl.BlockSpec(memory_space=pltpu.VMEM)
    s = pl.BlockSpec(memory_space=pltpu.SMEM)
    h = pl.BlockSpec(memory_space=pl.ANY)
    back, rows = pl.pallas_call(
        section_kernel,
        out_shape=(
            jax.ShapeDtypeStruct((32, 4, 16, 256), BF),
            jax.ShapeDtypeStruct((4, 32, 256), F32),
        ),
        in_specs=[h, h, h, h, h, v, s, s, h, h, h, h, h],
        out_specs=(v, v),
        scratch_shapes=scratch,
        compiler_params=pltpu.CompilerParams(
            collective_id=0, has_side_effects=True, vmem_limit_bytes=62 * 1024 * 1024
        ),
    )(
        pictures[0], taps, triple, final, upstream[0], slots.reshape(1, 128), counts, scaling,
        frame_rows(), gradient_rows(), column_shifts(), slot_expand(), head_sums(),
    )
    latents, conv_grad = pl.pallas_call(
        place_kernel,
        out_shape=(
            jax.ShapeDtypeStruct((4, 4, 128, 256), BF),
            jax.ShapeDtypeStruct((108, 256), F32),
        ),
        in_specs=[v, v, v],
        out_specs=(v, v),
    )(back, rows, result_rows())
    return latents[None], conv_grad


def solution(mesh):
    placed = (
        P("dp", "ctx", None, None, None, None),
        P(), P(), P(), P(), P(), P(),
        P("dp", "ctx", None, None, None),
    )
    return jax.shard_map(
        per_device,
        mesh=mesh,
        in_specs=placed,
        out_specs=(P("dp", "ctx", None, None, None), P("ctx", None)),
        check_vma=False,
    )
```

```python
import jax
import jax.numpy as jnp
import numpy as np
from jax import lax
from jax.experimental import pallas as pl
from jax.experimental.pallas import tpu as pltpu
from jax.sharding import PartitionSpec as P

BF = jnp.bfloat16
F32 = jnp.float32
MESH = pl.DeviceIdType.MESH
DEV = 32
UNROLL = 4
LOG2E = 1.4426950408889634


def one_hot_rows(rows, cols, pairs):
    table = np.zeros((rows, cols), np.float32)
    for row, col in pairs:
        table[row, col] = 1.0
    return jnp.asarray(table, BF)


def frame_rows():
    pairs = []
    for r in range(4):
        for qp in range(-1, 5):
            for k in range(4):
                for s in range(4):
                    q = qp + 4 * k
                    if 0 <= q < 16:
                        pairs.append((((r * 6 + qp + 1) * 4 + k) * 4 + s, (r * 4 + s) * 16 + q))
    return one_hot_rows(384, 256, pairs)


def gradient_rows():
    pairs = []
    for r in range(4):
        for qp in range(4):
            for k in range(4):
                for s in range(4):
                    pairs.append((((r * 4 + qp) * 4 + k) * 4 + s, (r * 4 + s) * 16 + qp + 4 * k))
    return one_hot_rows(256, 256, pairs)


def result_rows():
    pairs = []
    for qp in range(4):
        for k in range(4):
            for t in range(4):
                for s in range(4):
                    pairs.append(((s * 4 + t) * 16 + qp + 4 * k, ((qp * 4 + k) * 4 + t) * 4 + s))
    return one_hot_rows(256, 256, pairs)


def column_shifts():
    pairs = []
    for r in range(8):
        for k in range(4):
            for s in range(4):
                if k < 3:
                    pairs.append(((r * 4 + k) * 4 + s, (r * 4 + k + 1) * 4 + s))
                if k > 0:
                    pairs.append((128 + (r * 4 + k) * 4 + s, (r * 4 + k - 1) * 4 + s))
    return one_hot_rows(256, 128, pairs)


def slot_expand():
    pairs = []
    for e in range(32):
        for k in range(4):
            for s in range(4):
                pairs.append((4 * e + s, (e * 4 + k) * 4 + s))
    return one_hot_rows(128, 512, pairs)


def head_sums():
    table = np.kron(np.eye(4), np.ones((64, 64)))
    return jnp.asarray(table, BF)


def mm(a, b):
    return jnp.dot(a, b, preferred_element_type=F32)


def section_kernel(
    x_hbm, w_hbm, wqkv_hbm, wout_hbm, ug_hbm, sa_hbm, cnt_hbm, scale_hbm,
    px_hbm, pg_hbm, sh_hbm, ex_hbm, hs_hbm,
    back_ref, rows_ref,
    sa_ref, cnt_ref, scale_ref,
    x_ref, px_ref, ug_ref, pg_ref, w_ref, ex_ref, sh_ref, wqkv_ref, hs_ref, wout_ref,
    xp, xt, pat, t1r, t2s, t2r, cs, cr, gt, dwt, dw, gf, gbs, r1, s1b, r2, acc2, s2b, r3, s4,
    hot_t, hot_s, hot_u, mask, ys, qs, ks, vs, osb, rb,
    send_sem, recv_sem, red_send, red_recv, in_sem,
):
    z = lax.axis_index("dp")
    me = lax.axis_index("ctx")
    core = me & 1
    chip_x = (me >> 1) & 3
    chip_y = me >> 3

    loads = [
        pltpu.make_async_copy(source, target, in_sem.at[n])
        for n, (source, target) in enumerate((
            (x_hbm, x_ref), (px_hbm, px_ref), (ug_hbm, ug_ref), (pg_hbm, pg_ref), (w_hbm, w_ref), (ex_hbm, ex_ref),
            (sh_hbm, sh_ref), (wqkv_hbm, wqkv_ref), (hs_hbm, hs_ref), (wout_hbm, wout_ref),
            (sa_hbm, sa_ref), (cnt_hbm, cnt_ref), (scale_hbm, scale_ref),
        ))
    ]
    for load in loads[:2]:
        load.start()

    barrier = pltpu.get_barrier_semaphore()

    for step in range(1, DEV):
        peer = (me + step) & (DEV - 1)
        pl.semaphore_signal(barrier, inc=1, device_id={"ctx": peer}, device_id_type=MESH)
    for dz in range(1, 4):
        pl.semaphore_signal(barrier, inc=1, device_id={"dp": (z + dz) & 3}, device_id_type=MESH)
    for load in loads[2:]:
        load.start()

    def spread(source, target, phase):
        for step in range(1, DEV):
            peer = (me + step) & (DEV - 1)
            pltpu.make_async_remote_copy(
                src_ref=source(peer), dst_ref=target(me), send_sem=send_sem.at[phase],
                recv_sem=recv_sem.at[phase], device_id={"ctx": peer}, device_id_type=MESH,
            ).start()

    def landed(view, phase):
        pltpu.make_async_copy(view, view, recv_sem.at[phase]).wait()

    def left(view, phase):
        pltpu.make_async_copy(view, view, send_sem.at[phase]).wait()

    zero_rows = jnp.zeros((8, 6, 16, 128), BF)
    xp[:, 0] = zero_rows
    xp[:, 9] = zero_rows
    xt[:, 0] = zero_rows[:2]
    xt[:, 9] = zero_rows[:2]
    loads[0].wait()
    loads[1].wait()
    px = px_ref[...]
    def frames_in(pair):
        for g in range(2):
            rows = []
            for r in range(4 * g, 4 * g + 4):
                for s in range(4):
                    rows.append(
                        jnp.concatenate([x_ref[s, 2 * pair, r], x_ref[s, 2 * pair + 1, r]], axis=1)
                    )
            moved = mm(px, jnp.concatenate(rows, axis=0)).astype(BF)
            for f in range(2):
                xp[2 * pair + f, 1 + 4 * g : 5 + 4 * g] = moved[:, 128 * f : 128 * f + 128].reshape(4, 6, 16, 128)

    frames_in(3)
    pl.semaphore_wait(barrier, DEV - 1 + 3)
    my_r, my_q = me >> 2, me & 3
    spread(
        lambda peer: xp.at[pl.ds(6, 2), (peer >> 2) + 1, (peer & 3) + 1],
        lambda mine: t1r.at[:, mine],
        0,
    )
    t1r[:, me] = xp[6:8, my_r + 1, my_q + 1]
    for pair in (0, 1, 2):
        frames_in(pair)
    partner = me + 1 - 2 * core

    def reduce_copy(source, target, index, where):
        return pltpu.make_async_remote_copy(
            src_ref=source, dst_ref=target, send_sem=red_send.at[index],
            recv_sem=red_recv.at[index], device_id=where, device_id_type=MESH,
        )

    def regroup(g, carry):
        block = dw[pl.ds(pl.multiple_of(216 * g, 8), 224), :]
        for j in range(8):
            gf[j // 4, j % 4, g] = block[27 * j : 27 * j + 32]
        return carry

    def to_partner(first, last, index):
        lax.fori_loop(first, last, regroup, 0)
        for part in range(4):
            gbs[part, first:last] = gf[1 - core, part, first:last].astype(BF)
        span = pl.ds(first, last - first)
        copies = [
            reduce_copy(gbs.at[part, span], r1.at[part, span], index, {"ctx": partner}) for part in range(4)
        ]
        for copy in copies:
            copy.start()

    def to_planes(first, last, index):
        span = pl.ds(first, last - first)
        pltpu.make_async_copy(r1.at[:, span], r1.at[:, span], red_recv.at[index]).wait()
        for part in range(4):
            whole = gf[core, part, first:last] + r1[part, first:last].astype(F32)
            gf[core, part, first:last] = whole
            s1b[part, first:last] = whole.astype(BF)
        copies = [
            reduce_copy(s1b.at[(z + d) & 3, span], r2.at[d - 1, span], index + d, {"dp": (z + d) & 3}) for d in (1, 3, 2)
        ]
        for copy in copies:
            copy.start()
        return copies

    def taps(t, tail, kts):
        for kt in kts:
            for kh in range(3):
                for kw in range(3):
                    tap = (kt * 3 + kh) * 3 + kw
                    if tail:
                        tile = xt[kt, kh : kh + 8, kw : kw + 4]
                    else:
                        tile = xp[2 * t - 2 + kt, kh : kh + 8, kw : kw + 4]
                    pat[pl.ds(512 * t, 512), 128 * tap : 128 * tap + 128] = tile.reshape(512, 128)

    def convolve(t):
        for half in range(2):
            rows = pat[pl.ds(512 * t + 256 * half, 256), :]
            cs[pl.ds(16 * half, 16), t] = mm(rows, w_ref[...]).astype(BF).reshape(16, 16, 256)
        cr[me, t] = cs[me, t]

    def send_frame(t):
        spread(lambda peer: cs.at[peer, t], lambda mine: cr.at[mine, t], 2 + t)

    loads[4].wait()
    taps(1, False, (0, 1, 2))
    convolve(1)
    send_frame(1)
    loads[2].wait()
    loads[3].wait()
    pg = pg_ref[...]
    for t in range(4):
        for g in range(2):
            rows = []
            for r in range(4 * g, 4 * g + 4):
                for s in range(4):
                    rows.append(ug_ref[s, t, 16 * r : 16 * r + 16])
            moved = mm(pg, jnp.concatenate(rows, axis=0))
            at = (2 * t + g) * 256
            gt[:, at : at + 256] = jnp.transpose(moved).astype(BF)
    taps(2, False, (0, 1, 2))
    convolve(2)
    taps(3, False, (0, 1, 2))
    convolve(3)
    taps(0, False, (2,))

    for load in loads[10:]:
        load.wait()
    loads[5].wait()
    sa = sa_ref[...].astype(F32)
    opening = jnp.zeros((1, 128), jnp.bool_)
    first = jnp.int32(0)
    for n in range(16):
        opening = opening | (sa == first.astype(F32))
        first = first + cnt_ref[n]
    wanted = jnp.where(opening, -1000.0, sa * 4.0 - 4.0)
    codes = jnp.concatenate([sa * 4.0, wanted, jnp.zeros((14, 128), F32)], axis=0).astype(BF)
    wide = mm(codes, ex_ref[...])
    lane = lax.broadcasted_iota(jnp.int32, (1, 512), 1)
    kpat = ((lane >> 2) & 3).astype(F32)
    vrow = wide[0:1] + kpat
    wrow = wide[1:2] + kpat
    vcol = jnp.transpose(jnp.broadcast_to(vrow, (128, 512)))
    wcol = jnp.transpose(jnp.broadcast_to(wrow, (128, 512)))
    lane128 = lax.broadcasted_iota(jnp.int32, (1, 128), 1).astype(F32)
    for j in range(4):
        cols = slice(128 * j, 128 * j + 128)
        hot_t[:, cols] = jnp.where(wcol == vrow[:, cols], 1.0, 0.0).astype(BF)
        hot_u[:, cols] = jnp.where(vcol == lane128 * 4.0 + j, 1.0, 0.0).astype(BF)
        ids = lax.broadcasted_iota(jnp.int32, (128, 1), 0).astype(F32) * 4.0 + j
        hot_s[cols, :] = jnp.where(ids == vrow, 1.0, 0.0).astype(BF)

    def see(a, carry):
        row = lax.broadcasted_iota(jnp.int32, (128, 192), 0)
        col = lax.broadcasted_iota(jnp.int32, (128, 192), 1)
        span = 32 * a + (row & 31)
        when = span * 4 + (row >> 5)
        col_t = (col >= 48).astype(jnp.int32) + (col >= 96).astype(jnp.int32) + (col >= 144).astype(jnp.int32)
        other = 32 * a - 16 + col - 48 * col_t
        start = jnp.zeros((128, 192), jnp.int32)
        total = jnp.int32(0)
        for n in range(15):
            total = total + cnt_ref[n]
            start = jnp.where(span >= total, total, start)
        seen = (other >= start) & (other * 4 + col_t <= when)
        mask[a] = jnp.where(seen, 1.0, 0.0).astype(BF)
        return carry

    lax.fori_loop(0, 4, see, 0)
    ks[:, :, 0:16] = jnp.zeros((4, 4, 16, 256), BF)
    vs[:, :, :, 0:16, 0:128] = jnp.zeros((2, 4, 4, 16, 128), BF)
    vs[:, :, :, :, 128:256] = jnp.ones((2, 4, 4, 144, 128), BF)


    landed(t1r.at[:, pl.ds(0, DEV - 1)], 0)
    both = jnp.concatenate([t1r[0].reshape(512, 128), t1r[1].reshape(512, 128)], axis=1)
    moved = mm(hot_t[...], both).astype(BF)
    t2s[0] = moved[:, :128].reshape(32, 16, 128)
    t2s[1] = moved[:, 128:].reshape(32, 16, 128)
    spread(lambda peer: t2s.at[:, peer], lambda mine: t2r.at[:, mine], 1)
    t2r[:, me] = t2s[:, me]
    send_frame(2)

    def grad_last(n, carry):
        at = pl.multiple_of(2304 + n * 256, 256)
        dw[pl.ds(at, 256), :] = jnp.transpose(mm(gt[...], pat[:, pl.ds(at, 256)]))
        return carry

    lax.fori_loop(0, 4, grad_last, 0)
    dw[3328:3456, :] = jnp.transpose(mm(gt[...], pat[:, 3328:3456]))
    dw[3456:3464, :] = jnp.zeros((8, 256), F32)

    to_partner(11, 16, 0)

    def grad_main(n, carry):
        at = pl.multiple_of(n * 256, 256)
        dwt[:, pl.ds(at, 256)] = mm(gt[:, 512:2048], pat[512:2048, pl.ds(at, 256)])
        return carry

    lax.fori_loop(0, 3, grad_main, 0)
    send_frame(3)
    lax.fori_loop(3, 9, grad_main, 0)

    for load in loads[7:10]:
        load.wait()
    lanes = lax.broadcasted_iota(jnp.int32, (1, 256), 1)
    heads = [(lanes >> 6) == h for h in range(4)]
    left_half = lax.broadcasted_iota(jnp.int32, (1, 128), 1) < 64
    scale = jnp.zeros((1, 256), F32)
    for h in range(4):
        scale = jnp.where(heads[h], scale_ref[h] * LOG2E, scale)

    def stream_rows(t):
        landed(cr.at[pl.ds(0, DEV - 1), t], 2 + t)
        rows = mm(hot_s[...], cr[:, t].reshape(512, 256)).astype(BF)
        wide = rows.astype(F32)
        mean = jnp.mean(wide * wide, axis=1, keepdims=True)
        normed = (wide * lax.rsqrt(mean + 1e-6)).astype(BF)
        query = mm(normed, wqkv_ref[:, 0:256])
        sums = mm((query * query).astype(BF), hs_ref[...])
        query = (query * (lax.rsqrt(sums + 1e-6) * scale)).astype(BF)
        key = mm(normed, wqkv_ref[:, 256:512])
        sums = mm((key * key).astype(BF), hs_ref[...])
        key = (key * lax.rsqrt(sums + 1e-6)).astype(BF)
        value = mm(normed, wqkv_ref[:, 512:768]).astype(BF)
        for k in range(4):
            mine = slice(128 * k, 128 * k + 128)
            ys[k, t] = rows[mine]
            qs[k, t] = query[mine]
            ks[k, t, 16:144] = key[mine]
            for p in range(2):
                vs[p, k, t, 16:144, 0:128] = value[mine, 128 * p : 128 * p + 128]

    z_copies = to_planes(11, 16, 0)
    landed(t2r.at[:, pl.ds(0, DEV - 1)], 1)
    loads[6].wait()
    for f in range(2):
        tiles = t2r[f].reshape(8, 4, 16, 128)
        xt[f, 1:9, 1:5] = tiles
        up = mm(sh_ref[0:128], tiles[:, 0].reshape(128, 128)).astype(BF)
        down = mm(sh_ref[128:256], tiles[:, 3].reshape(128, 128)).astype(BF)
        xt[f, 1:9, 5] = up.reshape(8, 16, 128)
        xt[f, 1:9, 0] = down.reshape(8, 16, 128)
    taps(0, True, (0, 1))
    convolve(0)
    send_frame(0)

    def grad_tail(n, carry):
        at = pl.multiple_of(n * 256, 256)
        part = dwt[:, pl.ds(at, 256)] + mm(gt[:, 0:512], pat[0:512, pl.ds(at, 256)])
        dw[pl.ds(at, 256), :] = jnp.transpose(part)
        return carry

    lax.fori_loop(0, 9, grad_tail, 0, unroll=3)
    to_partner(0, 11, 4)


    stream_rows(1)
    stream_rows(2)
    z_copies += to_planes(0, 11, 4)
    stream_rows(3)
    def cell(k):
        def tile(a, carry):
            at = pl.multiple_of(32 * a, 32)
            see_a = jnp.concatenate([mask[a]] * 2, axis=0)
            joined = []
            for p in range(2):
                pair = slice(128 * p, 128 * p + 128)
                qa = jnp.concatenate([qs[k, t, pl.ds(at, 32), pair] for t in range(4)], axis=0)
                zero = jnp.zeros_like(qa)
                stacked = jnp.concatenate([jnp.where(left_half, qa, zero), jnp.where(left_half, zero, qa)], axis=0)
                keys = jnp.concatenate([ks[k, t, pl.ds(at, 48), pair] for t in range(4)], axis=0)
                vals = jnp.concatenate([vs[p, k, t, pl.ds(at, 48)] for t in range(4)], axis=0)
                scores = lax.dot_general(
                    stacked, keys, (((1,), (1,)), ((), ())), preferred_element_type=F32
                )
                weights = jnp.exp2(scores).astype(BF) * see_a
                both = mm(weights, vals)
                above_line = jnp.where(left_half, both[0:128, 0:128], both[128:256, 0:128])
                below_line = jnp.where(left_half, both[0:128, 128:256], both[128:256, 128:256])
                joined.append((above_line / below_line).astype(BF))
            joined = jnp.concatenate(joined, axis=1)
            base = jnp.concatenate([ys[k, t, pl.ds(at, 32)] for t in range(4)], axis=0)
            done = (base.astype(F32) + mm(joined, wout_ref[...])).astype(BF)
            for t in range(4):
                osb[t, pl.ds(at, 32)] = done[32 * t : 32 * t + 32]
            return carry

        lax.fori_loop(0, 4, tile, 0, unroll=UNROLL)

    def ship(k):
        back = mm(hot_u[...], osb[...].reshape(512, 256)).astype(BF)
        rb[k] = back.reshape(32, 16, 256)
        spread(lambda peer: rb.at[k, peer], lambda mine: back_ref.at[mine, k], 6 + k)
        back_ref[me, k] = rb[k, me]

    stream_rows(0)
    cell(0)
    ship(0)
    cell(1)
    ship(1)
    cell(2)

    for copy in z_copies:
        copy.wait()
    acc2[...] = gf[core, z] + r2[0].astype(F32) + r2[1].astype(F32) + r2[2].astype(F32)
    s2b[...] = acc2[...].astype(BF)
    chip = me >> 1
    plane_copies = []
    for d in range(1, 16):
        other = (chip + d) & 15
        plane_copies.append(reduce_copy(s2b.at[other], r3.at[d - 1], 8, {"ctx": other * 2 + core}))
    for copy in plane_copies:
        copy.start()
    ship(2)
    cell(3)
    ship(3)

    pltpu.make_async_copy(r3, r3, red_recv.at[8]).wait()
    total = acc2[chip]
    for d in range(15):
        total = total + r3[d].astype(F32)
    s4[...] = total
    end_copies = [
        reduce_copy(s4, rows_ref.at[z], 8 + d, {"dp": (z + d) & 3}) for d in (1, 2, 3)
    ]
    for copy in end_copies:
        copy.start()
    rows_ref[z] = s4[...]
    for k in range(4):
        landed(back_ref.at[pl.ds(0, DEV - 1), k], 6 + k)
    left(t1r.at[:, pl.ds(0, DEV - 1)], 0)
    left(t2s.at[:, pl.ds(0, DEV - 1)], 1)
    for t in range(4):
        left(cs.at[pl.ds(0, DEV - 1), t], 2 + t)
    for k in range(4):
        left(rb.at[k, pl.ds(0, DEV - 1)], 6 + k)
    pltpu.make_async_copy(r3, r3, red_send.at[8]).wait()
    for span, index in ((pl.ds(11, 5), 0), (pl.ds(0, 11), 4)):
        pltpu.make_async_copy(gbs.at[:, span], gbs.at[:, span], red_send.at[index]).wait()
    for copy in end_copies:
        copy.wait()


def place_kernel(back_ref, rows_ref, po_ref, out_ref, cg_ref):
    for r in range(8):
        moved = mm(po_ref[...], back_ref[4 * r : 4 * r + 4].reshape(256, 256)).astype(BF)
        for s in range(4):
            for t in range(4):
                at = (s * 4 + t) * 16
                out_ref[s, t, 16 * r : 16 * r + 16] = moved[at : at + 16]
    for part in range(4):
        cg_ref[27 * part : 27 * part + 27] = rows_ref[part, 0:27]


def per_device(pictures, slots, counts, scaling, taps, triple, final, upstream):
    vm = lambda shape, kind: pltpu.VMEM(shape, kind)
    scratch = [
        vm((1, 128), jnp.int32),
        pltpu.SMEM((16,), jnp.int32),
        pltpu.SMEM((4,), F32),
        vm((4, 8, 8, 16, 128), BF),
        vm((384, 256), BF),
        vm((4, 4, 128, 256), BF),
        vm((256, 256), BF),
        vm((3456, 256), BF),
        vm((128, 512), BF),
        vm((256, 128), BF),
        vm((256, 768), BF),
        vm((256, 256), BF),
        vm((256, 256), BF),
        vm((8, 10, 6, 16, 128), BF),
        vm((2, 10, 6, 16, 128), BF),
        vm((2048, 3456), BF),
        vm((2, 32, 16, 128), BF),
        vm((2, 32, 16, 128), BF),
        vm((2, 32, 16, 128), BF),
        vm((32, 4, 16, 256), BF),
        vm((32, 4, 16, 256), BF),
        vm((256, 2048), BF),
        vm((256, 2304), F32),
        vm((3464, 256), F32),
        vm((2, 4, 16, 32, 256), F32),
        vm((4, 16, 32, 256), BF),
        vm((4, 16, 32, 256), BF),
        vm((4, 16, 32, 256), BF),
        vm((3, 16, 32, 256), BF),
        vm((16, 32, 256), F32),
        vm((16, 32, 256), BF),
        vm((15, 32, 256), BF),
        vm((32, 256), F32),
        vm((512, 512), BF),
        vm((512, 512), BF),
        vm((512, 512), BF),
        vm((4, 128, 192), BF),
        vm((4, 4, 128, 256), BF),
        vm((4, 4, 128, 256), BF),
        vm((4, 4, 144, 256), BF),
        vm((2, 4, 4, 144, 256), BF),
        vm((4, 128, 256), BF),
        vm((4, 32, 16, 256), BF),
        pltpu.SemaphoreType.DMA((10,)),
        pltpu.SemaphoreType.DMA((10,)),
        pltpu.SemaphoreType.DMA((12,)),
        pltpu.SemaphoreType.DMA((12,)),
        pltpu.SemaphoreType.DMA((13,)),
    ]
    v = pl.BlockSpec(memory_space=pltpu.VMEM)
    h = pl.BlockSpec(memory_space=pl.ANY)
    back, rows = pl.pallas_call(
        section_kernel,
        out_shape=(
            jax.ShapeDtypeStruct((32, 4, 16, 256), BF),
            jax.ShapeDtypeStruct((4, 32, 256), F32),
        ),
        in_specs=[h] * 13,
        out_specs=(v, v),
        scratch_shapes=scratch,
        compiler_params=pltpu.CompilerParams(
            collective_id=0, has_side_effects=True, vmem_limit_bytes=62 * 1024 * 1024
        ),
    )(
        pictures[0], taps, triple, final, upstream[0], slots.reshape(1, 128), counts, scaling,
        frame_rows(), gradient_rows(), column_shifts(), slot_expand(), head_sums(),
    )
    latents, conv_grad = pl.pallas_call(
        place_kernel,
        out_shape=(
            jax.ShapeDtypeStruct((4, 4, 128, 256), BF),
            jax.ShapeDtypeStruct((108, 256), F32),
        ),
        in_specs=[v, v, v],
        out_specs=(v, v),
    )(back, rows, result_rows())
    return latents[None], conv_grad


def solution(mesh):
    placed = (
        P("dp", "ctx", None, None, None, None),
        P(), P(), P(), P(), P(), P(),
        P("dp", "ctx", None, None, None),
    )
    return jax.shard_map(
        per_device,
        mesh=mesh,
        in_specs=placed,
        out_specs=(P("dp", "ctx", None, None, None), P("ctx", None)),
        check_vma=False,
    )
```

```python
import jax
import jax.numpy as jnp
import numpy as np
from jax import lax
from jax.experimental import pallas as pl
from jax.experimental.pallas import tpu as pltpu
from jax.sharding import PartitionSpec as P

BF = jnp.bfloat16
F32 = jnp.float32
MESH = pl.DeviceIdType.MESH
DEV = 32
UNROLL = 4
LOG2E = 1.4426950408889634


def one_hot_rows(rows, cols, pairs):
    table = np.zeros((rows, cols), np.float32)
    for row, col in pairs:
        table[row, col] = 1.0
    return jnp.asarray(table, BF)


def frame_rows():
    pairs = []
    for r in range(4):
        for qp in range(-1, 5):
            for k in range(4):
                for s in range(4):
                    q = qp + 4 * k
                    if 0 <= q < 16:
                        pairs.append((((r * 6 + qp + 1) * 4 + k) * 4 + s, (r * 4 + s) * 16 + q))
    return one_hot_rows(384, 256, pairs)


def gradient_rows():
    pairs = []
    for r in range(4):
        for qp in range(4):
            for k in range(4):
                for s in range(4):
                    pairs.append((((r * 4 + qp) * 4 + k) * 4 + s, (r * 4 + s) * 16 + qp + 4 * k))
    return one_hot_rows(256, 256, pairs)


def result_rows():
    pairs = []
    for qp in range(4):
        for k in range(4):
            for t in range(4):
                for s in range(4):
                    pairs.append(((s * 4 + t) * 16 + qp + 4 * k, ((qp * 4 + k) * 4 + t) * 4 + s))
    return one_hot_rows(256, 256, pairs)


def column_shifts():
    pairs = []
    for r in range(8):
        for k in range(4):
            for s in range(4):
                if k < 3:
                    pairs.append(((r * 4 + k) * 4 + s, (r * 4 + k + 1) * 4 + s))
                if k > 0:
                    pairs.append((128 + (r * 4 + k) * 4 + s, (r * 4 + k - 1) * 4 + s))
    return one_hot_rows(256, 128, pairs)


def slot_expand():
    pairs = []
    for e in range(32):
        for k in range(4):
            for s in range(4):
                pairs.append((4 * e + s, (e * 4 + k) * 4 + s))
    return one_hot_rows(128, 512, pairs)


def head_sums():
    table = np.kron(np.eye(4), np.ones((64, 64)))
    return jnp.asarray(table, BF)


def mm(a, b):
    return jnp.dot(a, b, preferred_element_type=F32)


def section_kernel(
    x_hbm, w_hbm, wqkv_hbm, wout_hbm, ug_hbm, sa_hbm, cnt_hbm, scale_hbm,
    px_hbm, pg_hbm, sh_hbm, ex_hbm, hs_hbm,
    back_ref, rows_ref,
    sa_ref, cnt_ref, scale_ref,
    x_ref, px_ref, ug_ref, pg_ref, w_ref, ex_ref, sh_ref, wqkv_ref, hs_ref, wout_ref,
    xp, xt, pat, t1r, t2s, t2r, cs, cr, gt, dwt, dw, gf, gbs, r1, s1b, r2, acc2, s2b, r3, s4,
    hot_t, hot_s, hot_u, mask, ys, qs, ks, vs, osb, rb,
    send_sem, recv_sem, red_send, red_recv, in_sem,
):
    z = lax.axis_index("dp")
    me = lax.axis_index("ctx")
    core = me & 1
    chip_x = (me >> 1) & 3
    chip_y = me >> 3

    loads = [
        pltpu.make_async_copy(source, target, in_sem.at[n])
        for n, (source, target) in enumerate((
            (x_hbm, x_ref), (px_hbm, px_ref), (ug_hbm, ug_ref), (pg_hbm, pg_ref), (w_hbm, w_ref), (ex_hbm, ex_ref),
            (sh_hbm, sh_ref), (wqkv_hbm, wqkv_ref), (hs_hbm, hs_ref), (wout_hbm, wout_ref),
            (sa_hbm, sa_ref), (cnt_hbm, cnt_ref), (scale_hbm, scale_ref),
        ))
    ]
    for load in loads[:2]:
        load.start()

    barrier = pltpu.get_barrier_semaphore()

    for step in range(1, DEV):
        peer = (me + step) & (DEV - 1)
        pl.semaphore_signal(barrier, inc=1, device_id={"ctx": peer}, device_id_type=MESH)
    for dz in range(1, 4):
        pl.semaphore_signal(barrier, inc=1, device_id={"dp": (z + dz) & 3}, device_id_type=MESH)
    for load in loads[2:]:
        load.start()

    def spread(source, target, phase):
        for step in range(1, DEV):
            peer = (me + step) & (DEV - 1)
            pltpu.make_async_remote_copy(
                src_ref=source(peer), dst_ref=target(me), send_sem=send_sem.at[phase],
                recv_sem=recv_sem.at[phase], device_id={"ctx": peer}, device_id_type=MESH,
            ).start()

    def landed(view, phase):
        pltpu.make_async_copy(view, view, recv_sem.at[phase]).wait()

    def left(view, phase):
        pltpu.make_async_copy(view, view, send_sem.at[phase]).wait()

    zero_rows = jnp.zeros((8, 6, 16, 128), BF)
    xp[:, 0] = zero_rows
    xp[:, 9] = zero_rows
    xt[:, 0] = zero_rows[:2]
    xt[:, 9] = zero_rows[:2]
    loads[0].wait()
    loads[1].wait()
    px = px_ref[...]
    def frames_in(pair):
        for g in range(2):
            rows = []
            for r in range(4 * g, 4 * g + 4):
                for s in range(4):
                    rows.append(
                        jnp.concatenate([x_ref[s, 2 * pair, r], x_ref[s, 2 * pair + 1, r]], axis=1)
                    )
            moved = mm(px, jnp.concatenate(rows, axis=0)).astype(BF)
            for f in range(2):
                xp[2 * pair + f, 1 + 4 * g : 5 + 4 * g] = moved[:, 128 * f : 128 * f + 128].reshape(4, 6, 16, 128)

    frames_in(3)
    pl.semaphore_wait(barrier, DEV - 1 + 3)
    my_r, my_q = me >> 2, me & 3
    spread(
        lambda peer: xp.at[pl.ds(6, 2), (peer >> 2) + 1, (peer & 3) + 1],
        lambda mine: t1r.at[:, mine],
        0,
    )
    t1r[:, me] = xp[6:8, my_r + 1, my_q + 1]
    for pair in (0, 1, 2):
        frames_in(pair)
    partner = me + 1 - 2 * core

    def reduce_copy(source, target, index, where):
        return pltpu.make_async_remote_copy(
            src_ref=source, dst_ref=target, send_sem=red_send.at[index],
            recv_sem=red_recv.at[index], device_id=where, device_id_type=MESH,
        )

    def regroup(g, carry):
        block = dw[pl.ds(pl.multiple_of(216 * g, 8), 224), :]
        for j in range(8):
            gf[j // 4, j % 4, g] = block[27 * j : 27 * j + 32]
        return carry

    def to_partner(first, last, index):
        lax.fori_loop(first, last, regroup, 0)
        for part in range(4):
            gbs[part, first:last] = gf[1 - core, part, first:last].astype(BF)
        span = pl.ds(first, last - first)
        copies = [
            reduce_copy(gbs.at[part, span], r1.at[part, span], index, {"ctx": partner}) for part in range(4)
        ]
        for copy in copies:
            copy.start()

    def to_planes(first, last, index):
        span = pl.ds(first, last - first)
        pltpu.make_async_copy(r1.at[:, span], r1.at[:, span], red_recv.at[index]).wait()
        for part in range(4):
            whole = gf[core, part, first:last] + r1[part, first:last].astype(F32)
            gf[core, part, first:last] = whole
            s1b[part, first:last] = whole.astype(BF)
        copies = [
            reduce_copy(s1b.at[(z + d) & 3, span], r2.at[d - 1, span], index + d, {"dp": (z + d) & 3}) for d in (1, 3, 2)
        ]
        for copy in copies:
            copy.start()
        return copies

    def taps(t, tail, kts):
        for kt in kts:
            for kh in range(3):
                for kw in range(3):
                    tap = (kt * 3 + kh) * 3 + kw
                    if tail:
                        tile = xt[kt, kh : kh + 8, kw : kw + 4]
                    else:
                        tile = xp[2 * t - 2 + kt, kh : kh + 8, kw : kw + 4]
                    pat[pl.ds(512 * t, 512), 128 * tap : 128 * tap + 128] = tile.reshape(512, 128)

    def convolve(t):
        for half in range(2):
            rows = pat[pl.ds(512 * t + 256 * half, 256), :]
            cs[pl.ds(16 * half, 16), t] = mm(rows, w_ref[...]).astype(BF).reshape(16, 16, 256)
        cr[me, t] = cs[me, t]

    def send_frame(t):
        spread(lambda peer: cs.at[peer, t], lambda mine: cr.at[mine, t], 2 + t)

    loads[4].wait()
    taps(1, False, (0, 1, 2))
    convolve(1)
    send_frame(1)
    loads[2].wait()
    loads[3].wait()
    pg = pg_ref[...]
    for t in range(4):
        for g in range(2):
            rows = []
            for r in range(4 * g, 4 * g + 4):
                for s in range(4):
                    rows.append(ug_ref[s, t, 16 * r : 16 * r + 16])
            moved = mm(pg, jnp.concatenate(rows, axis=0))
            at = (2 * t + g) * 256
            gt[:, at : at + 256] = jnp.transpose(moved).astype(BF)
    taps(2, False, (0, 1, 2))
    convolve(2)
    taps(3, False, (0, 1, 2))
    convolve(3)
    taps(0, False, (2,))

    for load in loads[10:]:
        load.wait()
    loads[5].wait()
    sa = sa_ref[...].astype(F32)
    opening = jnp.zeros((1, 128), jnp.bool_)
    first = jnp.int32(0)
    for n in range(16):
        opening = opening | (sa == first.astype(F32))
        first = first + cnt_ref[n]
    wanted = jnp.where(opening, -1000.0, sa * 4.0 - 4.0)
    codes = jnp.concatenate([sa * 4.0, wanted, jnp.zeros((14, 128), F32)], axis=0).astype(BF)
    wide = mm(codes, ex_ref[...])
    lane = lax.broadcasted_iota(jnp.int32, (1, 512), 1)
    kpat = ((lane >> 2) & 3).astype(F32)
    vrow = wide[0:1] + kpat
    wrow = wide[1:2] + kpat
    vcol = jnp.transpose(jnp.broadcast_to(vrow, (128, 512)))
    wcol = jnp.transpose(jnp.broadcast_to(wrow, (128, 512)))
    lane128 = lax.broadcasted_iota(jnp.int32, (1, 128), 1).astype(F32)
    for j in range(4):
        cols = slice(128 * j, 128 * j + 128)
        hot_t[:, cols] = jnp.where(wcol == vrow[:, cols], 1.0, 0.0).astype(BF)
        hot_u[:, cols] = jnp.where(vcol == lane128 * 4.0 + j, 1.0, 0.0).astype(BF)
        ids = lax.broadcasted_iota(jnp.int32, (128, 1), 0).astype(F32) * 4.0 + j
        hot_s[cols, :] = jnp.where(ids == vrow, 1.0, 0.0).astype(BF)

    def see(a, carry):
        row = lax.broadcasted_iota(jnp.int32, (128, 192), 0)
        col = lax.broadcasted_iota(jnp.int32, (128, 192), 1)
        span = 32 * a + (row & 31)
        when = span * 4 + (row >> 5)
        col_t = (col >= 48).astype(jnp.int32) + (col >= 96).astype(jnp.int32) + (col >= 144).astype(jnp.int32)
        other = 32 * a - 16 + col - 48 * col_t
        start = jnp.zeros((128, 192), jnp.int32)
        total = jnp.int32(0)
        for n in range(15):
            total = total + cnt_ref[n]
            start = jnp.where(span >= total, total, start)
        seen = (other >= start) & (other * 4 + col_t <= when)
        mask[a] = jnp.where(seen, 1.0, 0.0).astype(BF)
        return carry

    lax.fori_loop(0, 4, see, 0)
    ks[:, :, 0:16] = jnp.zeros((4, 4, 16, 256), BF)
    vs[:, :, :, 0:16, 0:128] = jnp.zeros((2, 4, 4, 16, 128), BF)
    vs[:, :, :, :, 128:256] = jnp.ones((2, 4, 4, 144, 128), BF)


    landed(t1r.at[:, pl.ds(0, DEV - 1)], 0)
    both = jnp.concatenate([t1r[0].reshape(512, 128), t1r[1].reshape(512, 128)], axis=1)
    moved = mm(hot_t[...], both).astype(BF)
    t2s[0] = moved[:, :128].reshape(32, 16, 128)
    t2s[1] = moved[:, 128:].reshape(32, 16, 128)
    spread(lambda peer: t2s.at[:, peer], lambda mine: t2r.at[:, mine], 1)
    t2r[:, me] = t2s[:, me]
    send_frame(2)

    def grad_last(n, carry):
        at = pl.multiple_of(2304 + n * 256, 256)
        dw[pl.ds(at, 256), :] = jnp.transpose(mm(gt[...], pat[:, pl.ds(at, 256)]))
        return carry

    lax.fori_loop(0, 4, grad_last, 0, unroll=2)
    dw[3328:3456, :] = jnp.transpose(mm(gt[...], pat[:, 3328:3456]))
    dw[3456:3464, :] = jnp.zeros((8, 256), F32)

    to_partner(11, 16, 0)

    def grad_main(n, carry):
        at = pl.multiple_of(n * 256, 256)
        dwt[:, pl.ds(at, 256)] = mm(gt[:, 512:2048], pat[512:2048, pl.ds(at, 256)])
        return carry

    lax.fori_loop(0, 3, grad_main, 0, unroll=3)
    send_frame(3)
    lax.fori_loop(3, 9, grad_main, 0, unroll=3)

    for load in loads[7:10]:
        load.wait()
    lanes = lax.broadcasted_iota(jnp.int32, (1, 256), 1)
    heads = [(lanes >> 6) == h for h in range(4)]
    left_half = lax.broadcasted_iota(jnp.int32, (1, 128), 1) < 64
    scale = jnp.zeros((1, 256), F32)
    for h in range(4):
        scale = jnp.where(heads[h], scale_ref[h] * LOG2E, scale)

    def stream_rows(t):
        landed(cr.at[pl.ds(0, DEV - 1), t], 2 + t)
        rows = mm(hot_s[...], cr[:, t].reshape(512, 256)).astype(BF)
        wide = rows.astype(F32)
        mean = jnp.mean(wide * wide, axis=1, keepdims=True)
        normed = (wide * lax.rsqrt(mean + 1e-6)).astype(BF)
        query = mm(normed, wqkv_ref[:, 0:256])
        sums = mm((query * query).astype(BF), hs_ref[...])
        query = (query * (lax.rsqrt(sums + 1e-6) * scale)).astype(BF)
        key = mm(normed, wqkv_ref[:, 256:512])
        sums = mm((key * key).astype(BF), hs_ref[...])
        key = (key * lax.rsqrt(sums + 1e-6)).astype(BF)
        value = mm(normed, wqkv_ref[:, 512:768]).astype(BF)
        for k in range(4):
            mine = slice(128 * k, 128 * k + 128)
            ys[k, t] = rows[mine]
            qs[k, t] = query[mine]
            ks[k, t, 16:144] = key[mine]
            for p in range(2):
                vs[p, k, t, 16:144, 0:128] = value[mine, 128 * p : 128 * p + 128]

    z_copies = to_planes(11, 16, 0)
    landed(t2r.at[:, pl.ds(0, DEV - 1)], 1)
    loads[6].wait()
    for f in range(2):
        tiles = t2r[f].reshape(8, 4, 16, 128)
        xt[f, 1:9, 1:5] = tiles
        up = mm(sh_ref[0:128], tiles[:, 0].reshape(128, 128)).astype(BF)
        down = mm(sh_ref[128:256], tiles[:, 3].reshape(128, 128)).astype(BF)
        xt[f, 1:9, 5] = up.reshape(8, 16, 128)
        xt[f, 1:9, 0] = down.reshape(8, 16, 128)
    taps(0, True, (0, 1))
    convolve(0)
    send_frame(0)

    def grad_tail(n, carry):
        at = pl.multiple_of(n * 256, 256)
        part = dwt[:, pl.ds(at, 256)] + mm(gt[:, 0:512], pat[0:512, pl.ds(at, 256)])
        dw[pl.ds(at, 256), :] = jnp.transpose(part)
        return carry

    lax.fori_loop(0, 9, grad_tail, 0, unroll=3)
    to_partner(0, 11, 4)


    stream_rows(1)
    stream_rows(2)
    z_copies += to_planes(0, 11, 4)
    stream_rows(3)
    def cell(k):
        def tile(a, carry):
            at = pl.multiple_of(32 * a, 32)
            see_a = jnp.concatenate([mask[a]] * 2, axis=0)
            joined = []
            for p in range(2):
                pair = slice(128 * p, 128 * p + 128)
                qa = jnp.concatenate([qs[k, t, pl.ds(at, 32), pair] for t in range(4)], axis=0)
                zero = jnp.zeros_like(qa)
                stacked = jnp.concatenate([jnp.where(left_half, qa, zero), jnp.where(left_half, zero, qa)], axis=0)
                keys = jnp.concatenate([ks[k, t, pl.ds(at, 48), pair] for t in range(4)], axis=0)
                vals = jnp.concatenate([vs[p, k, t, pl.ds(at, 48)] for t in range(4)], axis=0)
                scores = lax.dot_general(
                    stacked, keys, (((1,), (1,)), ((), ())), preferred_element_type=F32
                )
                weights = jnp.exp2(scores).astype(BF) * see_a
                both = mm(weights, vals)
                above_line = jnp.where(left_half, both[0:128, 0:128], both[128:256, 0:128])
                below_line = jnp.where(left_half, both[0:128, 128:256], both[128:256, 128:256])
                joined.append((above_line / below_line).astype(BF))
            joined = jnp.concatenate(joined, axis=1)
            base = jnp.concatenate([ys[k, t, pl.ds(at, 32)] for t in range(4)], axis=0)
            done = (base.astype(F32) + mm(joined, wout_ref[...])).astype(BF)
            for t in range(4):
                osb[t, pl.ds(at, 32)] = done[32 * t : 32 * t + 32]
            return carry

        lax.fori_loop(0, 4, tile, 0, unroll=UNROLL)

    def ship(k):
        back = mm(hot_u[...], osb[...].reshape(512, 256)).astype(BF)
        rb[k] = back.reshape(32, 16, 256)
        spread(lambda peer: rb.at[k, peer], lambda mine: back_ref.at[mine, k], 6 + k)
        back_ref[me, k] = rb[k, me]

    stream_rows(0)
    cell(0)
    ship(0)
    cell(1)
    ship(1)
    cell(2)

    for copy in z_copies:
        copy.wait()
    acc2[...] = gf[core, z] + r2[0].astype(F32) + r2[1].astype(F32) + r2[2].astype(F32)
    s2b[...] = acc2[...].astype(BF)
    chip = me >> 1
    plane_copies = []
    for d in range(1, 16):
        other = (chip + d) & 15
        plane_copies.append(reduce_copy(s2b.at[other], r3.at[d - 1], 8, {"ctx": other * 2 + core}))
    for copy in plane_copies:
        copy.start()
    ship(2)
    cell(3)
    ship(3)

    pltpu.make_async_copy(r3, r3, red_recv.at[8]).wait()
    total = acc2[chip]
    for d in range(15):
        total = total + r3[d].astype(F32)
    s4[...] = total
    end_copies = [
        reduce_copy(s4, rows_ref.at[z], 8 + d, {"dp": (z + d) & 3}) for d in (1, 2, 3)
    ]
    for copy in end_copies:
        copy.start()
    rows_ref[z] = s4[...]
    for k in range(4):
        landed(back_ref.at[pl.ds(0, DEV - 1), k], 6 + k)
    left(t1r.at[:, pl.ds(0, DEV - 1)], 0)
    left(t2s.at[:, pl.ds(0, DEV - 1)], 1)
    for t in range(4):
        left(cs.at[pl.ds(0, DEV - 1), t], 2 + t)
    for k in range(4):
        left(rb.at[k, pl.ds(0, DEV - 1)], 6 + k)
    pltpu.make_async_copy(r3, r3, red_send.at[8]).wait()
    for span, index in ((pl.ds(11, 5), 0), (pl.ds(0, 11), 4)):
        pltpu.make_async_copy(gbs.at[:, span], gbs.at[:, span], red_send.at[index]).wait()
    for copy in end_copies:
        copy.wait()


def place_kernel(back_ref, rows_ref, po_ref, out_ref, cg_ref):
    for r in range(4):
        moved = mm(po_ref[...], back_ref[4 * r : 4 * r + 4].reshape(256, 256)).astype(BF)
        for s in range(4):
            for t in range(4):
                at = (s * 4 + t) * 16
                out_ref[s, t, 16 * r : 16 * r + 16] = moved[at : at + 16]
    for part in range(4):
        cg_ref[27 * part : 27 * part + 27] = rows_ref[part, 0:27]


def per_device(pictures, slots, counts, scaling, taps, triple, final, upstream):
    vm = lambda shape, kind: pltpu.VMEM(shape, kind)
    scratch = [
        vm((1, 128), jnp.int32),
        pltpu.SMEM((16,), jnp.int32),
        pltpu.SMEM((4,), F32),
        vm((4, 8, 8, 16, 128), BF),
        vm((384, 256), BF),
        vm((4, 4, 128, 256), BF),
        vm((256, 256), BF),
        vm((3456, 256), BF),
        vm((128, 512), BF),
        vm((256, 128), BF),
        vm((256, 768), BF),
        vm((256, 256), BF),
        vm((256, 256), BF),
        vm((8, 10, 6, 16, 128), BF),
        vm((2, 10, 6, 16, 128), BF),
        vm((2048, 3456), BF),
        vm((2, 32, 16, 128), BF),
        vm((2, 32, 16, 128), BF),
        vm((2, 32, 16, 128), BF),
        vm((32, 4, 16, 256), BF),
        vm((32, 4, 16, 256), BF),
        vm((256, 2048), BF),
        vm((256, 2304), F32),
        vm((3464, 256), F32),
        vm((2, 4, 16, 32, 256), F32),
        vm((4, 16, 32, 256), BF),
        vm((4, 16, 32, 256), BF),
        vm((4, 16, 32, 256), BF),
        vm((3, 16, 32, 256), BF),
        vm((16, 32, 256), F32),
        vm((16, 32, 256), BF),
        vm((15, 32, 256), BF),
        vm((32, 256), F32),
        vm((512, 512), BF),
        vm((512, 512), BF),
        vm((512, 512), BF),
        vm((4, 128, 192), BF),
        vm((4, 4, 128, 256), BF),
        vm((4, 4, 128, 256), BF),
        vm((4, 4, 144, 256), BF),
        vm((2, 4, 4, 144, 256), BF),
        vm((4, 128, 256), BF),
        vm((4, 32, 16, 256), BF),
        pltpu.SemaphoreType.DMA((10,)),
        pltpu.SemaphoreType.DMA((10,)),
        pltpu.SemaphoreType.DMA((12,)),
        pltpu.SemaphoreType.DMA((12,)),
        pltpu.SemaphoreType.DMA((13,)),
    ]
    v = pl.BlockSpec(memory_space=pltpu.VMEM)
    h = pl.BlockSpec(memory_space=pl.ANY)
    back, rows = pl.pallas_call(
        section_kernel,
        out_shape=(
            jax.ShapeDtypeStruct((32, 4, 16, 256), BF),
            jax.ShapeDtypeStruct((4, 32, 256), F32),
        ),
        in_specs=[h] * 13,
        out_specs=(v, v),
        scratch_shapes=scratch,
        compiler_params=pltpu.CompilerParams(
            collective_id=0, has_side_effects=True, vmem_limit_bytes=62 * 1024 * 1024
        ),
    )(
        pictures[0], taps, triple, final, upstream[0], slots.reshape(1, 128), counts, scaling,
        frame_rows(), gradient_rows(), column_shifts(), slot_expand(), head_sums(),
    )
    latents, conv_grad = pl.pallas_call(
        place_kernel,
        out_shape=(
            jax.ShapeDtypeStruct((4, 4, 128, 256), BF),
            jax.ShapeDtypeStruct((108, 256), F32),
        ),
        grid=(2,),
        in_specs=[
            pl.BlockSpec((16, 4, 16, 256), lambda n: (n, 0, 0, 0)),
            pl.BlockSpec((4, 32, 256), lambda n: (0, 0, 0)),
            pl.BlockSpec((256, 256), lambda n: (0, 0)),
        ],
        out_specs=(
            pl.BlockSpec((4, 4, 64, 256), lambda n: (0, 0, n, 0)),
            pl.BlockSpec((108, 256), lambda n: (0, 0)),
        ),
    )(back, rows, result_rows())
    return latents[None], conv_grad


def solution(mesh):
    placed = (
        P("dp", "ctx", None, None, None, None),
        P(), P(), P(), P(), P(), P(),
        P("dp", "ctx", None, None, None),
    )
    return jax.shard_map(
        per_device,
        mesh=mesh,
        in_specs=placed,
        out_specs=(P("dp", "ctx", None, None, None), P("ctx", None)),
        check_vma=False,
    )
```
